32 devices in a mesh: band: 8 (over z, y), lev: 4 (over x, core).
Axes of the slice: x: 2, y: 2, z: 4, core: 2. Of those that a mesh axis runs over, the one named last changes fastest.
Arguments:
- winds: float32 [3, 4, 262144], P(None, 'lev', 'band'), may hold values from -6 to 6
- remap_w: float32 [4, 8, 4096], P(None, 'band'), may hold values from 0.1 to 1
- remap_col: int32 [4, 8, 4096], P(None, 'band'), may hold values from 0 to 1535
- block_pick: int32 [8, 96], replicated, may hold values from 0 to 255
- cycle_ids: int32 [8], P('band'), may hold values from 1024 to 3072
- wave_ids: int32 [2048], replicated, may hold values from 0 to 2047, each once
- legendre_a: bfloat16 [2048, 8, 2048], P(('band', 'lev')), may hold values from -0.03125 to 0.03125
- legendre_b: bfloat16 [2048, 8, 2048], P(('band', 'lev')), may hold values from -0.03125 to 0.03125
Outputs:
- divergence: float32 [2, 4, 2048, 2048], P(None, None, ('band', 'lev'))
- vorticity: float32 [2, 4, 2048, 2048], P(None, None, ('band', 'lev'))
The draws below stay inside these ranges and needn't reach their ends.
Inputs may be any that keep to these rules, and one draw needn't show every extreme that they name: `block_pick`: block indices within one column shard. `remap_col`: offsets within the 12 picked blocks of one source column shard. `cycle_ids`: Equatorial-belt cycle numbers. `wave_ids`: each wavenumber below 2048 once.
All inputs are finite; a program needn't handle non-finite values.
Results may differ from the reference program's by a relative error of at most 0.0029.
Values may be sent and summed in bfloat16 or wider, within the bound.
No kernel may reach another device: no remote copies, remote signals or barrier semaphores. Data moves between devices by JAX's collectives and lax.ppermute only.
A program may use at most 192 MiB of HBM per device.

```python
import math
import jax
import jax.numpy as jnp
from jax import lax

NSIDE = 1024
NPHI = 4096
M = 2048
L = 2048
K = 4
BLK = 128
PER = 12
SB_DEV = 256
CYCLE_DEV = 1
LEVELS = 4
CYCLES = 8
COLS = 262144
N_BAND = 8


def place_ends(array, own_key, smallest, largest):
    longest = array.shape.index(max(array.shape))
    spots = []
    for shift in (0, 1):
        where = [jax.random.randint(jax.random.fold_in(own_key, axis), (), 0, length) for axis, length in enumerate(array.shape)]
        where[longest] = (where[longest] + shift) % array.shape[longest]
        spots.append(tuple(where))
    return array.at[spots[0]].set(smallest).at[spots[1]].set(largest)


def steps_of(own_key, dims, shards, low, top_value):
    factor_of = 1.0
    for dim, shards_of in shards:
        steps = jax.random.uniform(jax.random.fold_in(jax.random.fold_in(own_key, 6), dim), (shards_of,), jnp.float32, low / len(shards), top_value / len(shards))
        factor_of = factor_of * jnp.repeat(jnp.exp(steps), dims[dim] // shards_of).reshape((-1,) + (1,) * (len(dims) - 1 - dim))
    return factor_of


def noise(rng, dims, scale, bound, split=(), kind=jnp.bfloat16):
    factor_of = steps_of(rng, dims, split, -0.22, 0.18) if split else 1.0
    array = jax.random.normal(rng, dims, jnp.float32) * scale * factor_of
    return jnp.minimum(jnp.maximum(array, -bound), bound).astype(kind)


def setup_inputs(seed: int = 0) -> dict:
    key_list = jax.random.split(jax.random.key(seed), 9)
    return {
        "winds": noise(key_list[0], (3, LEVELS, COLS), 1.0, 6.0, ((1, 4), (2, 8)), jnp.float32),
        "remap_w": jnp.clip(jnp.exp(math.log(1.0) - 2.3025851 * jax.random.uniform(key_list[1], (K, CYCLES, NPHI), jnp.float32) ** steps_of(key_list[1], (K, CYCLES, NPHI), ((1, 8),), -0.2, 0.2)), 0.1, 1.0),
        "remap_col": place_ends(jax.random.randint(key_list[2], (K, CYCLES, NPHI), 0, PER * BLK), jax.random.fold_in(key_list[2], 1), 0, (PER * BLK) - 1).astype(jnp.int32),
        "block_pick": place_ends(jax.random.randint(key_list[3], (N_BAND, N_BAND * PER), 0, SB_DEV), jax.random.fold_in(key_list[3], 1), 0, SB_DEV - 1).astype(jnp.int32),
        "cycle_ids": place_ends(jax.random.randint(key_list[4], (CYCLES,), NSIDE, 3 * NSIDE + 1), jax.random.fold_in(key_list[4], 1), NSIDE, 3 * NSIDE).astype(jnp.int32),
        "wave_ids": jax.random.permutation(key_list[5], M).astype(jnp.int32),
        "legendre_a": noise(key_list[6], (M, CYCLES, L), (CYCLES * NPHI) ** -0.5, 0.03125, ((0, 32),)),
        "legendre_b": noise(key_list[7], (M, CYCLES, L), (CYCLES * NPHI) ** -0.5, 0.03125, ((0, 32),)),
    }


def geometry(cycle_number, nside):
    cycle_float = cycle_number.astype(jnp.float32)
    cos_theta = 4.0 / 3.0 - 2.0 * cycle_float / (3.0 * nside)
    sin_theta = jnp.sqrt(1.0 - cos_theta * cos_theta)
    half_shift = ((cycle_number - nside + 1) % 2).astype(jnp.float32)
    return (cos_theta, sin_theta, half_shift)

def reference(winds, remap_w, remap_col, block_pick, cycle_ids, wave_ids, legendre_a, legendre_b):
    cycle_slot = jnp.arange(CYCLES, dtype=jnp.int32)[:, None]
    position = jnp.arange(NPHI, dtype=jnp.int32)[None, :]
    target = cycle_slot // CYCLE_DEV
    pixel = cycle_slot % CYCLE_DEV * NPHI + position
    source = pixel % N_BAND
    picked = block_pick[target[None], source[None] * PER + remap_col // BLK]
    column = source[None] * (SB_DEV * BLK) + picked * BLK + remap_col % BLK
    sampled = winds[:, :, column]
    cartesian = lax.optimization_barrier(jnp.sum(sampled * remap_w[None, None], axis=2))
    cos_theta, sin_theta, half_shift = geometry(cycle_ids, NSIDE)
    spacing = math.pi / (2.0 * NSIDE)
    azimuth = spacing * (position.astype(jnp.float32) + 1.0 - 0.5 * half_shift[:, None])
    cos_phi = jnp.cos(azimuth)
    sin_phi = jnp.sin(azimuth)
    east = -sin_phi * cartesian[0] + cos_phi * cartesian[1]
    north = -cos_theta[:, None] * (cos_phi * cartesian[0] + sin_phi * cartesian[1]) + sin_theta[:, None] * cartesian[2]
    spectra = jnp.fft.rfft(jnp.stack([east, north]), axis=-1)[..., :M]
    raw_real = jnp.real(spectra).astype(jnp.float32)
    raw_imag = jnp.imag(spectra).astype(jnp.float32)
    start = spacing * (1.0 - 0.5 * half_shift)
    angle = start[:, None] * jnp.arange(M, dtype=jnp.int32).astype(jnp.float32)[None, :]
    cos_rot = jnp.cos(angle)
    sin_rot = jnp.sin(angle)
    rot_real = raw_real * cos_rot + raw_imag * sin_rot
    rot_imag = raw_imag * cos_rot - raw_real * sin_rot
    modes = jnp.stack([rot_real[0], rot_imag[0], rot_real[1], rot_imag[1]], axis=1).astype(jnp.bfloat16)
    chosen = jnp.take(modes, wave_ids, axis=3)
    slot_rows = jnp.transpose(chosen, (3, 0, 1, 2)).reshape(M, LEVELS * 4, CYCLES)
    degree = jnp.arange(L, dtype=jnp.int32)

    def one_slot(item):
        mode_rows, table_a, table_b, wavenumber = item
        part_a = jnp.dot(mode_rows, table_a, preferred_element_type=jnp.float32).reshape(LEVELS, 4, L)
        part_b = jnp.dot(mode_rows, table_b, preferred_element_type=jnp.float32).reshape(LEVELS, 4, L)
        upper = (degree >= wavenumber)[None, :]
        div_real = jnp.where(upper, -part_a[:, 1] - part_b[:, 2], 0.0)
        div_imag = jnp.where(upper, part_a[:, 0] - part_b[:, 3], 0.0)
        vort_real = jnp.where(upper, -part_a[:, 3] + part_b[:, 0], 0.0)
        vort_imag = jnp.where(upper, part_a[:, 2] + part_b[:, 1], 0.0)
        return (jnp.stack([div_real, div_imag]), jnp.stack([vort_real, vort_imag]))
    div_all, vort_all = lax.map(one_slot, (slot_rows, legendre_a, legendre_b, wave_ids))
    return (jnp.transpose(div_all, (1, 2, 0, 3)), jnp.transpose(vort_all, (1, 2, 0, 3)))
```

```python
import functools
import math

import jax
import jax.numpy as jnp
import numpy as np
from jax import lax
from jax.experimental import pallas as pl
from jax.experimental.pallas import tpu as pltpu
from jax.sharding import PartitionSpec as P

BLK = 128
LANES = 128
SUB = 8
HIGHEST = lax.Precision.HIGHEST


def pick_kernel(picks, winds, out, *, per):
    band = lax.axis_index("band")
    components = winds.shape[0]

    def one_target(t, carry):
        for c in range(per):
            block = picks[t, band * per + c]
            for comp in range(components):
                out[t, pl.ds(comp * per + c, 1), :] = winds[comp, pl.ds(block, 1), :]
        return carry

    lax.fori_loop(0, out.shape[0], one_target, 0, unroll=out.shape[0] <= 8)


def pick_blocks(block_pick, winds, band_count, per):
    components, blocks, _ = winds.shape
    return pl.pallas_call(
        functools.partial(pick_kernel, per=per),
        out_shape=jax.ShapeDtypeStruct((band_count, components * per, BLK), winds.dtype),
        in_specs=[
            pl.BlockSpec(memory_space=pltpu.SMEM),
            pl.BlockSpec(memory_space=pltpu.VMEM),
        ],
        out_specs=pl.BlockSpec(memory_space=pltpu.VMEM),
        name="pick",
    )(block_pick, winds)


@functools.lru_cache(maxsize=None)
def tables(cycle_length, taps, waves):
    rows = cycle_length // LANES
    b = np.arange(LANES, dtype=np.int64)
    lane_r = np.arange(taps * rows, dtype=np.int64) % rows
    p = np.arange(LANES, dtype=np.int64)
    u = np.arange(waves // LANES, dtype=np.int64)
    turn = 2.0 * np.pi
    azimuth = turn / cycle_length * (LANES * lane_r[None, :] + b[:, None] + 1)
    outer = turn / rows * (lane_r[:, None] * p[None, :] % rows)
    twist = turn / cycle_length * (b[:, None] * p[None, :] % cycle_length)
    inner = turn * ((LANES * u[:, None] * b[None, :]) % cycle_length) / cycle_length
    half_turn = turn / (2 * cycle_length) * (LANES * u[:, None] + p[None, :])
    f32 = np.float32
    return dict(
        azimuth=np.stack([np.cos(azimuth), np.sin(azimuth)]).astype(f32),
        outer=np.concatenate([np.cos(outer), -np.sin(outer)], 1).astype(f32),
        twist=np.stack([np.cos(twist), np.sin(twist)]).astype(f32),
        inner=np.block(
            [[np.cos(inner), np.sin(inner)], [-np.sin(inner), np.cos(inner)]]
        ).astype(f32),
        start=np.stack([np.cos(half_turn), np.sin(half_turn)]).astype(f32),
    )


def modes_kernel(
    cycle, received, col, weight, order, azimuth, outer, twist, inner, start, out, col_t, weight_t,
    cart, field, *, per, nside, paired
):
    band_count = received.shape[0]
    components = received.shape[1] // per
    tiles = LANES // SUB
    groups = band_count // SUB
    col_t[...] = jnp.transpose(col[...])
    weight_t[...] = jnp.transpose(weight[...])
    for comp in range(components):
        for group in range(groups):
            block_rows = [
                received[group * SUB : (group + 1) * SUB, comp * per + blk, :] for blk in range(per)
            ]
            for tile in range(group, tiles, groups):
                index = col_t[tile * SUB : (tile + 1) * SUB, :]
                lane = index & (BLK - 1)
                block = index >> (BLK.bit_length() - 1)
                value = jnp.take_along_axis(block_rows[0], lane, axis=1)
                for blk in range(1, per):
                    value = jnp.where(
                        block == blk, jnp.take_along_axis(block_rows[blk], lane, axis=1), value
                    )
                cart[comp, tile * SUB : (tile + 1) * SUB, :] = (
                    value * weight_t[tile * SUB : (tile + 1) * SUB, :]
                )
    number = cycle[0]
    half = lax.rem(number - nside + 1, 2) != 0
    spacing = math.pi / (2.0 * nside)
    turn_cos = jnp.where(half, math.cos(0.5 * spacing), 1.0).astype(jnp.float32)
    turn_sin = jnp.where(half, math.sin(0.5 * spacing), 0.0).astype(jnp.float32)
    number_f = jnp.full((SUB, LANES), number, jnp.int32).astype(jnp.float32)
    cos_tile = 4.0 / 3.0 - 2.0 * number_f / (3.0 * nside)
    sin_tile = jnp.sqrt(1.0 - cos_tile * cos_tile)
    cos_theta = cos_tile[:1, :]
    sin_theta = sin_tile[:1, :]
    cos_phi = azimuth[0] * turn_cos + azimuth[1] * turn_sin
    sin_phi = azimuth[1] * turn_cos - azimuth[0] * turn_sin
    x, y, z = cart[0], cart[1], cart[2]
    east = cos_phi * y - sin_phi * x
    north = sin_theta * z - cos_theta * (cos_phi * x + sin_phi * y)
    samples = jnp.concatenate([east, north], axis=0)
    section = jnp.dot(samples, outer[...], precision=HIGHEST, preferred_element_type=jnp.float32)
    turned_real = []
    turned_imag = []
    for f in range(2):
        real = section[f * LANES : (f + 1) * LANES, :LANES]
        imag = section[f * LANES : (f + 1) * LANES, LANES:]
        turned_real.append(real * twist[0] + imag * twist[1])
        turned_imag.append(imag * twist[0] - real * twist[1])
    turned = jnp.concatenate(
        [jnp.concatenate(turned_real, axis=1), jnp.concatenate(turned_imag, axis=1)], axis=0
    )
    spectrum = jnp.dot(inner[...], turned, precision=HIGHEST, preferred_element_type=jnp.float32)
    rows = start.shape[1]
    half_cos, half_sin = start[0], start[1]
    rot_cos = jnp.where(half, half_cos, half_cos * half_cos - half_sin * half_sin)
    rot_sin = jnp.where(half, half_sin, 2.0 * half_cos * half_sin)
    for f in range(2):
        real = spectrum[:rows, f * LANES : (f + 1) * LANES]
        imag = spectrum[rows:, f * LANES : (f + 1) * LANES]
        field[2 * f] = real * rot_cos + imag * rot_sin
        field[2 * f + 1] = imag * rot_cos - real * rot_sin
    low = lax.broadcasted_iota(jnp.int32, (SUB, LANES), 1) < LANES // 2
    for top in range(0, rows, SUB):
        wave = order[top : top + SUB, :]
        lane = wave & (LANES - 1)
        block = wave >> (LANES.bit_length() - 1)
        picked = []
        for k in range(4):
            value = None
            for blk in range(rows):
                source = jnp.broadcast_to(field[k, blk : blk + 1, :], (SUB, LANES))
                found = jnp.take_along_axis(source, lane, axis=1)
                value = found if value is None else jnp.where(block == blk, found, value)
            picked.append(value.astype(jnp.bfloat16).astype(jnp.float32))
        if paired:
            for h in range(2):
                first, second = picked[2 * h], picked[2 * h + 1]
                out[top : top + SUB, h, :] = jnp.where(
                    low, first, pltpu.roll(second, LANES // 2, axis=1)
                )
                out[top : top + SUB, 2 + h, :] = jnp.where(
                    low, pltpu.roll(first, LANES // 2, axis=1), second
                )
        else:
            for k in range(4):
                out[top : top + SUB, k, :] = picked[k]


def cycle_modes(cycle_ids, received, col, weight, order, taps, cycle_length, waves, per, paired):
    table = tables(cycle_length, taps, waves)
    names = ("azimuth", "outer", "twist", "inner", "start")
    components = received.shape[1] // per
    rows = waves // LANES
    vmem = pl.BlockSpec(memory_space=pltpu.VMEM)
    return pl.pallas_call(
        functools.partial(modes_kernel, per=per, nside=cycle_length // 4, paired=paired),
        out_shape=jax.ShapeDtypeStruct((rows, 4, LANES), jnp.float32),
        in_specs=[pl.BlockSpec(memory_space=pltpu.SMEM)] + [vmem] * 9,
        out_specs=vmem,
        scratch_shapes=[
            pltpu.VMEM((LANES, LANES), jnp.int32),
            pltpu.VMEM((LANES, LANES), jnp.float32),
            pltpu.VMEM((components, LANES, LANES), jnp.float32),
            pltpu.VMEM((4, rows, LANES), jnp.float32),
        ],
        name="modes",
    )(cycle_ids, received, col, weight, order, *[jnp.asarray(table[n]) for n in names])


PARTS = ((-1, 1, -1, 2), (1, 0, -1, 3), (-1, 3, 1, 0), (1, 2, 1, 1))


def legendre_kernel(modes, first_wave, table_a, table_b, div, vort, spread, *, levels, cycles, group, split):
    step = pl.program_id(0)
    owned = spread.shape[1]
    width = group * cycles

    @pl.when(step == 0)
    def _():
        rows = modes.shape[0]
        row = lax.broadcasted_iota(jnp.int32, (rows, levels * split * width), 0)
        lane = lax.broadcasted_iota(jnp.int32, (rows, levels * split * width), 1)
        same = (lax.rem(row, levels * split) == lax.div(lane, width)) & (
            lax.div(row, levels * split) == lax.rem(lane, cycles)
        )
        pick = jnp.where(same, 1.0, 0.0).astype(jnp.bfloat16)
        turned = jnp.transpose(modes[...]).astype(jnp.bfloat16)
        wide = jnp.dot(turned, pick, preferred_element_type=jnp.float32)
        slot = lax.broadcasted_iota(jnp.int32, (owned, width), 0)
        place = lax.broadcasted_iota(jnp.int32, (owned, width), 1)
        own = lax.rem(slot, group) == lax.div(place, cycles)
        for f in range(4):
            h, i = divmod(f, 4 // split)
            for lev in range(levels):
                start = (lev * split + h) * width
                part = wide[i * owned : (i + 1) * owned, start : start + width]
                spread[f * levels + lev] = jnp.where(own, part, 0.0).astype(jnp.bfloat16)

    base = pl.multiple_of(step * group, group)
    pieces = []
    for sign_a, field_a, sign_b, field_b in PARTS:
        for lev in range(levels):
            left = spread[field_a * levels + lev, pl.ds(base, group), :]
            right = spread[field_b * levels + lev, pl.ds(base, group), :]
            left = left if sign_a > 0 else -left
            right = right if sign_b > 0 else -right
            pieces.append(jnp.concatenate([left, right], axis=1))
    mix = jnp.concatenate(pieces, axis=0)
    degrees = table_a.shape[1]
    chunk = min(256, degrees)
    waves = first_wave[pl.ds(base, group), :]
    for start in range(0, degrees, chunk):
        both = jnp.concatenate(
            [table_a[:, start : start + chunk], table_b[:, start : start + chunk]], axis=0
        )
        result = jnp.dot(mix, both, preferred_element_type=jnp.float32)
        for at in range(0, chunk, LANES):
            degree = lax.broadcasted_iota(jnp.int32, (group, LANES), 1) + (start + at)
            upper = degree >= waves
            for part in range(4):
                target = div if part < 2 else vort
                for lev in range(levels):
                    top = (part * levels + lev) * group
                    target[part % 2, lev, :, start + at : start + at + LANES] = jnp.where(
                        upper, result[top : top + group, at : at + LANES], 0.0
                    )


def legendre_sums(modes, first_wave, legendre_a, legendre_b, levels, split):
    owned, cycles, degrees = legendre_a.shape
    group = math.gcd(owned, 16)
    flat = (owned * cycles, degrees)
    table_spec = pl.BlockSpec((group * cycles, degrees), lambda i: (i, 0))
    out_spec = pl.BlockSpec((2, levels, group, degrees), lambda i: (0, 0, i, 0))
    out_shape = jax.ShapeDtypeStruct((2, levels, owned, degrees), jnp.float32)
    return pl.pallas_call(
        functools.partial(
            legendre_kernel, levels=levels, cycles=cycles, group=group, split=split
        ),
        grid=(owned // group,),
        out_shape=(out_shape, out_shape),
        in_specs=[
            pl.BlockSpec(modes.shape, lambda i: (0, 0)),
            pl.BlockSpec(first_wave.shape, lambda i: (0, 0)),
            table_spec,
            table_spec,
        ],
        out_specs=(out_spec, out_spec),
        scratch_shapes=[pltpu.VMEM((4 * levels, owned, group * cycles), jnp.bfloat16)],
        name="legendre",
    )(modes, first_wave, legendre_a.reshape(flat), legendre_b.reshape(flat))


def local(winds, remap_w, remap_col, block_pick, cycle_ids, wave_ids, legendre_a, legendre_b):
    band_count = lax.axis_size("band")
    level_count = lax.axis_size("lev")
    components, levels_dev, column_count = winds.shape
    taps, cycle_count, cycle_length = remap_col.shape
    per = block_pick.shape[1] // band_count
    waves = wave_ids.shape[0]
    devices = band_count * level_count
    owned = waves // devices
    assert levels_dev == 1 and cycle_count == 1
    assert taps * cycle_length == LANES * LANES and band_count % SUB == 0
    blocks = winds.reshape(components, column_count // BLK, BLK)
    outgoing = pick_blocks(block_pick, blocks, band_count, per)
    received = lax.all_to_all(outgoing, "band", split_axis=0, concat_axis=0, tiled=True)
    paired = 2 * owned == LANES
    chosen = cycle_modes(
        cycle_ids,
        received,
        remap_col.reshape(LANES, LANES),
        remap_w.reshape(LANES, LANES),
        wave_ids.reshape(waves // LANES, LANES),
        taps,
        cycle_length,
        waves,
        per,
        paired,
    )
    split = 2 if paired else 1
    if paired:
        parcels = chosen.reshape(devices, split, LANES)
    else:
        parcels = jnp.transpose(
            jnp.transpose(chosen, (1, 0, 2)).reshape(4, devices, owned), (1, 0, 2)
        ).reshape(devices, 1, 4 * owned)
    gathered = lax.all_to_all(parcels, ("band", "lev"), split_axis=0, concat_axis=0, tiled=True)
    modes = gathered.reshape(devices * split, 4 * owned // split)
    slot_start = (lax.axis_index("band") * level_count + lax.axis_index("lev")) * owned
    my_waves = lax.dynamic_slice_in_dim(wave_ids, slot_start, owned)
    first_wave = jnp.broadcast_to(my_waves[:, None], (owned, LANES))
    return legendre_sums(modes, first_wave, legendre_a, legendre_b, level_count, split)


def solution(mesh):
    placed = (
        P(None, "lev", "band"),
        P(None, "band", None),
        P(None, "band", None),
        P(),
        P("band"),
        P(),
        P(("band", "lev"), None, None),
        P(("band", "lev"), None, None),
    )
    return jax.shard_map(
        local,
        mesh=mesh,
        in_specs=placed,
        out_specs=(P(None, None, ("band", "lev"), None), P(None, None, ("band", "lev"), None)),
        check_vma=False,
    )
```

```python
import functools
import math

import jax
import jax.numpy as jnp
import numpy as np
from jax import lax
from jax.experimental import pallas as pl
from jax.experimental.pallas import tpu as pltpu
from jax.sharding import PartitionSpec as P

BLK = 128
LANES = 128
SUB = 8
VMEM_ALL = 67043328
ROOM = 12000 * 1024
HIGHEST = lax.Precision.HIGHEST


def pick_kernel(picks, winds, out, *, per):
    band = lax.axis_index("band")
    components = winds.shape[0]

    def one_target(t, carry):
        for c in range(per):
            block = picks[t, band * per + c]
            for comp in range(components):
                place, row = divmod(comp * per + c, out.shape[2])
                out[t, place, pl.ds(row, 1), :] = winds[comp, pl.ds(block, 1), :]
        return carry

    lax.fori_loop(0, out.shape[0], one_target, 0, unroll=out.shape[0] <= 8)


def pick_blocks(block_pick, winds, band_count, per):
    components, blocks, _ = winds.shape
    quad = math.gcd(components * per, 4)
    return pl.pallas_call(
        functools.partial(pick_kernel, per=per),
        out_shape=jax.ShapeDtypeStruct(
            (band_count, components * per // quad, quad, BLK), winds.dtype
        ),
        in_specs=[
            pl.BlockSpec(memory_space=pltpu.SMEM),
            pl.BlockSpec(memory_space=pltpu.VMEM),
        ],
        out_specs=pl.BlockSpec(memory_space=pltpu.VMEM),
        compiler_params=pltpu.CompilerParams(vmem_limit_bytes=VMEM_ALL),
        name="pick",
    )(block_pick, winds)


@functools.lru_cache(maxsize=None)
def tables(cycle_length, taps, waves):
    rows = cycle_length // LANES
    b = np.arange(LANES, dtype=np.int64)
    lane_r = np.arange(taps * rows, dtype=np.int64) % rows
    p = np.arange(LANES, dtype=np.int64)
    u = np.arange(waves // LANES, dtype=np.int64)
    turn = 2.0 * np.pi
    azimuth = turn / cycle_length * (LANES * lane_r[None, :] + b[:, None] + 1)
    outer = turn / rows * (lane_r[:, None] * p[None, :] % rows)
    twist = turn / cycle_length * (b[:, None] * p[None, :] % cycle_length)
    inner = turn * ((LANES * u[:, None] * b[None, :]) % cycle_length) / cycle_length
    half_turn = turn / (2 * cycle_length) * (LANES * u[:, None] + p[None, :])
    f32 = np.float32
    parts = dict(
        cos_phi=np.cos(azimuth),
        sin_phi=np.sin(azimuth),
        outer_real=np.cos(outer),
        outer_imag=-np.sin(outer),
        twist_cos=np.cos(twist),
        twist_sin=np.sin(twist),
        inner_real=np.concatenate([np.cos(inner), -np.sin(inner)], 0),
        inner_imag=np.concatenate([np.sin(inner), np.cos(inner)], 0),
        half_cos=np.cos(half_turn),
        half_sin=np.sin(half_turn),
    )
    spans = {}
    top = 0
    for name, part in parts.items():
        spans[name] = slice(top, top + part.shape[0])
        top += part.shape[0]
    spans["rest"] = slice(spans["outer_real"].start, top)
    return np.concatenate(list(parts.values()), 0).astype(np.float32), spans


def geometry_kernel(
    cycle, col, weight, order, table_hbm, col_t, weight_t, turn_cos, turn_sin, first_wave, rest,
    order_near, line, sems, *, spans, nside
):
    cos_phi = pltpu.make_async_copy(table_hbm.at[spans["cos_phi"], :], turn_cos, sems.at[0])
    sin_phi = pltpu.make_async_copy(table_hbm.at[spans["sin_phi"], :], turn_sin, sems.at[1])
    other = pltpu.make_async_copy(table_hbm.at[spans["rest"], :], rest, sems.at[2])
    cos_phi.start()
    sin_phi.start()
    other.start()
    col_t[...] = jnp.transpose(col[...])
    weight_t[...] = jnp.transpose(weight[...])
    order_near[...] = order[...]
    owned = first_wave.shape[0]
    slot = (lax.axis_index("band") * lax.axis_size("lev") + lax.axis_index("lev")) * owned
    mine = order[pl.ds(lax.div(slot, LANES), 1), :]
    line[...] = jnp.transpose(jnp.broadcast_to(mine, (LANES, LANES)))
    first_wave[...] = line[pl.ds(pl.multiple_of(lax.rem(slot, LANES), SUB), owned), :]
    half = lax.rem(cycle[0] - nside + 1, 2) != 0
    spacing = math.pi / (2.0 * nside)
    shift_cos = jnp.where(half, math.cos(0.5 * spacing), 1.0).astype(jnp.float32)
    shift_sin = jnp.where(half, math.sin(0.5 * spacing), 0.0).astype(jnp.float32)
    cos_phi.wait()
    sin_phi.wait()
    base_cos, base_sin = turn_cos[...], turn_sin[...]
    turn_cos[...] = base_cos * shift_cos + base_sin * shift_sin
    turn_sin[...] = base_sin * shift_cos - base_cos * shift_sin
    other.wait()


def cycle_geometry(cycle_ids, col, weight, order, owned, cycle_length, table, spans):
    vmem = pl.BlockSpec(memory_space=pltpu.VMEM)
    square = (LANES, LANES)
    rest = spans["rest"].stop - spans["rest"].start
    return pl.pallas_call(
        functools.partial(geometry_kernel, spans=spans, nside=cycle_length // 4),
        out_shape=(
            jax.ShapeDtypeStruct(square, jnp.int32),
            jax.ShapeDtypeStruct(square, jnp.float32),
            jax.ShapeDtypeStruct(square, jnp.float32),
            jax.ShapeDtypeStruct(square, jnp.float32),
            jax.ShapeDtypeStruct((owned, LANES), jnp.int32),
            jax.ShapeDtypeStruct((rest, LANES), jnp.float32),
            jax.ShapeDtypeStruct(order.shape, jnp.int32),
        ),
        in_specs=[pl.BlockSpec(memory_space=pltpu.SMEM), vmem, vmem, vmem]
        + [pl.BlockSpec(memory_space=pltpu.HBM)],
        out_specs=(vmem,) * 7,
        scratch_shapes=[pltpu.VMEM(square, jnp.int32), pltpu.SemaphoreType.DMA((3,))],
        compiler_params=pltpu.CompilerParams(vmem_limit_bytes=VMEM_ALL - ROOM),
        cost_estimate=pl.CostEstimate(flops=10**7, bytes_accessed=10**7, transcendentals=0),
        name="geometry",
    )(cycle_ids, col, weight, order, table)


def modes_kernel(
    cycle, received, col_t, weight_t, turn_cos, turn_sin, order, table, out, cart, field,
    *, spans, per, nside, paired
):
    band_count, _, quad, _ = received.shape
    components = cart.shape[0]
    tiles = LANES // SUB
    groups = band_count // SUB
    first = spans["rest"].start

    def part(name):
        return table[spans[name].start - first : spans[name].stop - first, :]

    for comp in range(components):
        for group in range(groups):
            block_rows = [
                received[(slice(group * SUB, (group + 1) * SUB), *divmod(comp * per + blk, quad))]
                for blk in range(per)
            ]
            for tile in range(group, tiles, groups):
                index = col_t[tile * SUB : (tile + 1) * SUB, :]
                lane = index & (BLK - 1)
                block = index >> (BLK.bit_length() - 1)
                value = jnp.take_along_axis(block_rows[0], lane, axis=1)
                for blk in range(1, per):
                    value = jnp.where(
                        block == blk, jnp.take_along_axis(block_rows[blk], lane, axis=1), value
                    )
                cart[comp, tile * SUB : (tile + 1) * SUB, :] = (
                    value * weight_t[tile * SUB : (tile + 1) * SUB, :]
                )
    number = cycle[0]
    half = lax.rem(number - nside + 1, 2) != 0
    number_f = jnp.full((SUB, LANES), number, jnp.int32).astype(jnp.float32)
    cos_tile = 4.0 / 3.0 - 2.0 * number_f / (3.0 * nside)
    sin_tile = jnp.sqrt(1.0 - cos_tile * cos_tile)
    cos_theta = cos_tile[:1, :]
    sin_theta = sin_tile[:1, :]
    cos_phi, sin_phi = turn_cos[...], turn_sin[...]
    x, y, z = cart[0], cart[1], cart[2]
    east = cos_phi * y - sin_phi * x
    north = sin_theta * z - cos_theta * (cos_phi * x + sin_phi * y)
    samples = jnp.concatenate([east, north], axis=0)
    outer = jnp.concatenate([part("outer_real"), part("outer_imag")], axis=1)
    section = jnp.dot(samples, outer, precision=HIGHEST, preferred_element_type=jnp.float32)
    twist_cos, twist_sin = part("twist_cos"), part("twist_sin")
    turned_real = []
    turned_imag = []
    for f in range(2):
        real = section[f * LANES : (f + 1) * LANES, :LANES]
        imag = section[f * LANES : (f + 1) * LANES, LANES:]
        turned_real.append(real * twist_cos + imag * twist_sin)
        turned_imag.append(imag * twist_cos - real * twist_sin)
    turned = jnp.concatenate(
        [jnp.concatenate(turned_real, axis=1), jnp.concatenate(turned_imag, axis=1)], axis=0
    )
    inner = jnp.concatenate([part("inner_real"), part("inner_imag")], axis=1)
    spectrum = jnp.dot(inner, turned, precision=HIGHEST, preferred_element_type=jnp.float32)
    rows = field.shape[1]
    half_cos, half_sin = part("half_cos"), part("half_sin")
    rot_cos = jnp.where(half, half_cos, half_cos * half_cos - half_sin * half_sin)
    rot_sin = jnp.where(half, half_sin, 2.0 * half_cos * half_sin)
    for f in range(2):
        real = spectrum[:rows, f * LANES : (f + 1) * LANES]
        imag = spectrum[rows:, f * LANES : (f + 1) * LANES]
        field[2 * f] = real * rot_cos + imag * rot_sin
        field[2 * f + 1] = imag * rot_cos - real * rot_sin
    low = lax.broadcasted_iota(jnp.int32, (SUB, LANES), 1) < LANES // 2
    for top in range(0, rows, SUB):
        wave = order[top : top + SUB, :]
        lane = wave & (LANES - 1)
        block = wave >> (LANES.bit_length() - 1)
        picked = []
        for k in range(4):
            value = None
            for blk in range(rows):
                source = jnp.broadcast_to(field[k, blk : blk + 1, :], (SUB, LANES))
                found = jnp.take_along_axis(source, lane, axis=1)
                value = found if value is None else jnp.where(block == blk, found, value)
            picked.append(value.astype(jnp.bfloat16).astype(jnp.float32))
        if paired:
            for h in range(2):
                first_f, second_f = picked[2 * h], picked[2 * h + 1]
                out[top : top + SUB, h, :] = jnp.where(
                    low, first_f, pltpu.roll(second_f, LANES // 2, axis=1)
                )
                out[top : top + SUB, 2 + h, :] = jnp.where(
                    low, pltpu.roll(first_f, LANES // 2, axis=1), second_f
                )
        else:
            for k in range(4):
                out[top : top + SUB, k, :] = picked[k]


def cycle_modes(cycle_ids, received, geometry, components, cycle_length, per, paired, spans):
    col_t, weight_t, turn_cos, turn_sin, _, rest, order = geometry
    rows = order.shape[0]
    vmem = pl.BlockSpec(memory_space=pltpu.VMEM)
    return pl.pallas_call(
        functools.partial(
            modes_kernel, spans=spans, per=per, nside=cycle_length // 4, paired=paired
        ),
        out_shape=jax.ShapeDtypeStruct((rows, 4, LANES), jnp.float32),
        in_specs=[pl.BlockSpec(memory_space=pltpu.SMEM)] + [vmem] * 7,
        out_specs=vmem,
        scratch_shapes=[
            pltpu.VMEM((components, LANES, LANES), jnp.float32),
            pltpu.VMEM((4, rows, LANES), jnp.float32),
        ],
        compiler_params=pltpu.CompilerParams(vmem_limit_bytes=VMEM_ALL - ROOM),
        name="modes",
    )(cycle_ids, received, col_t, weight_t, turn_cos, turn_sin, order, rest)


PARTS = ((-1, 1, -1, 2), (1, 0, -1, 3), (-1, 3, 1, 0), (1, 2, 1, 1))


def legendre_kernel(
    modes, first_wave, a_hbm, b_hbm, div_hbm, vort_hbm, table_a, table_b, spread, div, vort, in_sems,
    out_sems, *, levels, cycles, group, split
):
    owned = spread.shape[1]
    width = group * cycles
    groups = owned // group
    degrees = table_a.shape[1]

    def fetch(g, which):
        source, target = ((a_hbm, table_a), (b_hbm, table_b))[which]
        rows = pl.ds(g * width, width)
        return pltpu.make_async_copy(source.at[rows, :], target.at[rows, :], in_sems.at[g, which])

    def flush(g, which):
        source, target = ((div, div_hbm), (vort, vort_hbm))[which]
        rows = pl.ds(g * group, group)
        return pltpu.make_async_copy(
            source.at[:, :, rows, :], target.at[:, :, rows, :], out_sems.at[g, which]
        )

    for g in range(groups):
        for which in range(2):
            fetch(g, which).start()
    rows = modes.shape[0]
    row = lax.broadcasted_iota(jnp.int32, (rows, levels * split * width), 0)
    lane = lax.broadcasted_iota(jnp.int32, (rows, levels * split * width), 1)
    same = (lax.rem(row, levels * split) == lax.div(lane, width)) & (
        lax.div(row, levels * split) == lax.rem(lane, cycles)
    )
    pick = jnp.where(same, 1.0, 0.0).astype(jnp.bfloat16)
    turned = jnp.transpose(modes[...]).astype(jnp.bfloat16)
    wide = jnp.dot(turned, pick, preferred_element_type=jnp.float32)
    slot = lax.broadcasted_iota(jnp.int32, (owned, width), 0)
    place = lax.broadcasted_iota(jnp.int32, (owned, width), 1)
    own = lax.rem(slot, group) == lax.div(place, cycles)
    for f in range(4):
        h, i = divmod(f, 4 // split)
        for lev in range(levels):
            start = (lev * split + h) * width
            part = wide[i * owned : (i + 1) * owned, start : start + width]
            spread[f * levels + lev] = jnp.where(own, part, 0.0).astype(jnp.bfloat16)
    chunk = min(256, degrees)
    for g in range(groups):
        base = g * group
        pieces = []
        for sign_a, field_a, sign_b, field_b in PARTS:
            for lev in range(levels):
                left = spread[field_a * levels + lev, base : base + group, :]
                right = spread[field_b * levels + lev, base : base + group, :]
                left = left if sign_a > 0 else -left
                right = right if sign_b > 0 else -right
                pieces.append(jnp.concatenate([left, right], axis=1))
        mix = jnp.concatenate(pieces, axis=0)
        waves = first_wave[base : base + group, :]
        fetch(g, 0).wait()
        fetch(g, 1).wait()
        for start in range(0, degrees, chunk):
            at_rows = slice(g * width, (g + 1) * width)
            both = jnp.concatenate(
                [table_a[at_rows, start : start + chunk], table_b[at_rows, start : start + chunk]],
                axis=0,
            )
            result = jnp.dot(mix, both, preferred_element_type=jnp.float32)
            for at in range(0, chunk, LANES):
                degree = lax.broadcasted_iota(jnp.int32, (group, LANES), 1) + (start + at)
                upper = degree >= waves
                for part in range(4):
                    target = div if part < 2 else vort
                    for lev in range(levels):
                        top = (part * levels + lev) * group
                        lanes = slice(start + at, start + at + LANES)
                        target[part % 2, lev, base : base + group, lanes] = jnp.where(
                            upper, result[top : top + group, at : at + LANES], 0.0
                        )
        flush(g, 0).start()
        flush(g, 1).start()
    for g in range(groups):
        flush(g, 0).wait()
        flush(g, 1).wait()


def legendre_sums(modes, first_wave, legendre_a, legendre_b, levels, split):
    owned, cycles, degrees = legendre_a.shape
    group = math.gcd(owned, 16)
    flat = (owned * cycles, degrees)
    full = (2, levels, owned, degrees)
    out_shape = jax.ShapeDtypeStruct(full, jnp.float32)
    vmem = pl.BlockSpec(memory_space=pltpu.VMEM)
    hbm = pl.BlockSpec(memory_space=pltpu.HBM)
    return pl.pallas_call(
        functools.partial(
            legendre_kernel, levels=levels, cycles=cycles, group=group, split=split
        ),
        out_shape=(out_shape, out_shape),
        in_specs=[vmem, vmem, hbm, hbm],
        out_specs=(hbm, hbm),
        scratch_shapes=[
            pltpu.VMEM(flat, jnp.bfloat16),
            pltpu.VMEM(flat, jnp.bfloat16),
            pltpu.VMEM((4 * levels, owned, group * cycles), jnp.bfloat16),
            pltpu.VMEM(full, jnp.float32),
            pltpu.VMEM(full, jnp.float32),
            pltpu.SemaphoreType.DMA((owned // group, 2)),
            pltpu.SemaphoreType.DMA((owned // group, 2)),
        ],
        compiler_params=pltpu.CompilerParams(vmem_limit_bytes=VMEM_ALL - ROOM),
        name="legendre",
    )(modes, first_wave, legendre_a.reshape(flat), legendre_b.reshape(flat))


def local(winds, remap_w, remap_col, block_pick, cycle_ids, wave_ids, legendre_a, legendre_b):
    band_count = lax.axis_size("band")
    level_count = lax.axis_size("lev")
    components, levels_dev, column_count = winds.shape
    taps, cycle_count, cycle_length = remap_col.shape
    per = block_pick.shape[1] // band_count
    waves = wave_ids.shape[0]
    devices = band_count * level_count
    owned = waves // devices
    assert levels_dev == 1 and cycle_count == 1
    assert taps * cycle_length == LANES * LANES and band_count % SUB == 0
    blocks = winds.reshape(components, column_count // BLK, BLK)
    outgoing = pick_blocks(block_pick, blocks, band_count, per)
    received = lax.all_to_all(outgoing, "band", split_axis=0, concat_axis=0, tiled=True)
    paired = 2 * owned == LANES
    table, spans = tables(cycle_length, taps, waves)
    order = wave_ids.reshape(waves // LANES, LANES)
    geometry = cycle_geometry(
        cycle_ids,
        remap_col.reshape(LANES, LANES),
        remap_w.reshape(LANES, LANES),
        order,
        owned,
        cycle_length,
        jnp.asarray(table),
        spans,
    )
    chosen = cycle_modes(
        cycle_ids, received, geometry, components, cycle_length, per, paired, spans
    )
    first_wave = geometry[4]
    split = 2 if paired else 1
    if paired:
        parcels = chosen.reshape(devices, split, LANES)
    else:
        parcels = jnp.transpose(
            jnp.transpose(chosen, (1, 0, 2)).reshape(4, devices, owned), (1, 0, 2)
        ).reshape(devices, 1, 4 * owned)
    gathered = lax.all_to_all(parcels, ("band", "lev"), split_axis=0, concat_axis=0, tiled=True)
    modes = gathered.reshape(devices * split, 4 * owned // split)
    return legendre_sums(modes, first_wave, legendre_a, legendre_b, level_count, split)


def solution(mesh):
    placed = (
        P(None, "lev", "band"),
        P(None, "band", None),
        P(None, "band", None),
        P(),
        P("band"),
        P(),
        P(("band", "lev"), None, None),
        P(("band", "lev"), None, None),
    )
    return jax.shard_map(
        local,
        mesh=mesh,
        in_specs=placed,
        out_specs=(P(None, None, ("band", "lev"), None), P(None, None, ("band", "lev"), None)),
        check_vma=False,
    )
```

```python
import functools
import math

import jax
import jax.numpy as jnp
import numpy as np
from jax import lax
from jax.experimental import pallas as pl
from jax.experimental.pallas import tpu as pltpu
from jax.sharding import PartitionSpec as P

BLK = 128
LANES = 128
SUB = 8
GROUP = 16
EARLY = 2
VMEM_ALL = 67043328
ROOM = 24000 * 1024
HIGHEST = lax.Precision.HIGHEST


def far(array):
    return pltpu.with_memory_space_constraint(array, pltpu.HBM)


def pick_kernel(picks, winds, out, *, per):
    band = lax.axis_index("band")
    components = winds.shape[0]

    def one_target(t, carry):
        for c in range(per):
            block = picks[t, band * per + c]
            for comp in range(components):
                place, row = divmod(comp * per + c, out.shape[2])
                out[t, place, pl.ds(row, 1), :] = winds[comp, pl.ds(block, 1), :]
        return carry

    lax.fori_loop(0, out.shape[0], one_target, 0, unroll=out.shape[0] <= 8)


def pick_blocks(block_pick, winds, band_count, per):
    components, blocks, _ = winds.shape
    quad = math.gcd(components * per, 4)
    return pl.pallas_call(
        functools.partial(pick_kernel, per=per),
        out_shape=jax.ShapeDtypeStruct(
            (band_count, components * per // quad, quad, BLK), winds.dtype
        ),
        in_specs=[
            pl.BlockSpec(memory_space=pltpu.SMEM),
            pl.BlockSpec(memory_space=pltpu.VMEM),
        ],
        out_specs=pl.BlockSpec(memory_space=pltpu.VMEM),
        compiler_params=pltpu.CompilerParams(vmem_limit_bytes=VMEM_ALL - ROOM),
        name="pick",
    )(far(block_pick), far(winds))


@functools.lru_cache(maxsize=None)
def tables(cycle_length, taps, waves):
    rows = cycle_length // LANES
    b = np.arange(LANES, dtype=np.int64)
    lane_r = np.arange(taps * rows, dtype=np.int64) % rows
    p = np.arange(LANES, dtype=np.int64)
    u = np.arange(waves // LANES, dtype=np.int64)
    turn = 2.0 * np.pi
    azimuth = turn / cycle_length * (LANES * lane_r[None, :] + b[:, None] + 1)
    outer = turn / rows * (lane_r[:, None] * p[None, :] % rows)
    twist = turn / cycle_length * (b[:, None] * p[None, :] % cycle_length)
    inner = turn * ((LANES * u[:, None] * b[None, :]) % cycle_length) / cycle_length
    half_turn = turn / (2 * cycle_length) * (LANES * u[:, None] + p[None, :])
    f32 = np.float32
    parts = dict(
        cos_phi=np.cos(azimuth),
        sin_phi=np.sin(azimuth),
        outer_real=np.cos(outer),
        outer_imag=-np.sin(outer),
        twist_cos=np.cos(twist),
        twist_sin=np.sin(twist),
        inner_real=np.concatenate([np.cos(inner), -np.sin(inner)], 0),
        inner_imag=np.concatenate([np.sin(inner), np.cos(inner)], 0),
        half_cos=np.cos(half_turn),
        half_sin=np.sin(half_turn),
    )
    spans = {}
    top = 0
    for name, part in parts.items():
        spans[name] = slice(top, top + part.shape[0])
        top += part.shape[0]
    spans["rest"] = slice(spans["outer_real"].start, top)
    return np.concatenate(list(parts.values()), 0).astype(np.float32), spans


def early_shape(flat, owned):
    group = math.gcd(owned, GROUP)
    return (2, min(EARLY, owned // group) * group * (flat[0] // owned), flat[1])


def geometry_kernel(
    cycle, col, weight, order, table_hbm, a_hbm, b_hbm, col_t, weight_t, turn_cos, turn_sin,
    first_wave, rest, order_near, early, line, sems, *, spans, nside
):
    rows = early.shape[1]
    early_a = pltpu.make_async_copy(a_hbm.at[:rows, :], early.at[0], sems.at[3])
    early_b = pltpu.make_async_copy(b_hbm.at[:rows, :], early.at[1], sems.at[4])
    cos_phi = pltpu.make_async_copy(table_hbm.at[spans["cos_phi"], :], turn_cos, sems.at[0])
    sin_phi = pltpu.make_async_copy(table_hbm.at[spans["sin_phi"], :], turn_sin, sems.at[1])
    other = pltpu.make_async_copy(table_hbm.at[spans["rest"], :], rest, sems.at[2])
    cos_phi.start()
    sin_phi.start()
    other.start()
    early_a.start()
    early_b.start()
    col_t[...] = jnp.transpose(col[...])
    weight_t[...] = jnp.transpose(weight[...])
    order_near[...] = order[...]
    owned = first_wave.shape[0]
    slot = (lax.axis_index("band") * lax.axis_size("lev") + lax.axis_index("lev")) * owned
    mine = order[pl.ds(lax.div(slot, LANES), 1), :]
    line[...] = jnp.transpose(jnp.broadcast_to(mine, (LANES, LANES)))
    first_wave[...] = line[pl.ds(pl.multiple_of(lax.rem(slot, LANES), SUB), owned), :]
    half = lax.rem(cycle[0] - nside + 1, 2) != 0
    spacing = math.pi / (2.0 * nside)
    shift_cos = jnp.where(half, math.cos(0.5 * spacing), 1.0).astype(jnp.float32)
    shift_sin = jnp.where(half, math.sin(0.5 * spacing), 0.0).astype(jnp.float32)
    cos_phi.wait()
    sin_phi.wait()
    base_cos, base_sin = turn_cos[...], turn_sin[...]
    turn_cos[...] = base_cos * shift_cos + base_sin * shift_sin
    turn_sin[...] = base_sin * shift_cos - base_cos * shift_sin
    other.wait()
    early_a.wait()
    early_b.wait()


def cycle_geometry(cycle_ids, col, weight, order, owned, cycle_length, table, spans, flat_a, flat_b):
    vmem = pl.BlockSpec(memory_space=pltpu.VMEM)
    square = (LANES, LANES)
    rest = spans["rest"].stop - spans["rest"].start
    return pl.pallas_call(
        functools.partial(geometry_kernel, spans=spans, nside=cycle_length // 4),
        out_shape=(
            jax.ShapeDtypeStruct(square, jnp.int32),
            jax.ShapeDtypeStruct(square, jnp.float32),
            jax.ShapeDtypeStruct(square, jnp.float32),
            jax.ShapeDtypeStruct(square, jnp.float32),
            jax.ShapeDtypeStruct((owned, LANES), jnp.int32),
            jax.ShapeDtypeStruct((rest, LANES), jnp.float32),
            jax.ShapeDtypeStruct(order.shape, jnp.int32),
            jax.ShapeDtypeStruct(early_shape(flat_a.shape, owned), flat_a.dtype),
        ),
        in_specs=[pl.BlockSpec(memory_space=pltpu.SMEM), vmem, vmem, vmem]
        + [pl.BlockSpec(memory_space=pltpu.HBM)] * 3,
        out_specs=(vmem,) * 8,
        scratch_shapes=[pltpu.VMEM(square, jnp.int32), pltpu.SemaphoreType.DMA((5,))],
        compiler_params=pltpu.CompilerParams(vmem_limit_bytes=VMEM_ALL - ROOM),
        cost_estimate=pl.CostEstimate(flops=10**7, bytes_accessed=10**7, transcendentals=0),
        name="geometry",
    )(cycle_ids, *[far(x) for x in (col, weight, order, table, flat_a, flat_b)])


def modes_kernel(
    cycle, received, col_t, weight_t, turn_cos, turn_sin, order, table, out, cart, field,
    *, spans, per, nside, paired
):
    band_count, _, quad, _ = received.shape
    components = cart.shape[0]
    tiles = LANES // SUB
    groups = band_count // SUB
    first = spans["rest"].start

    def part(name):
        return table[spans[name].start - first : spans[name].stop - first, :]

    for comp in range(components):
        for group in range(groups):
            block_rows = [
                received[(slice(group * SUB, (group + 1) * SUB), *divmod(comp * per + blk, quad))]
                for blk in range(per)
            ]
            for tile in range(group, tiles, groups):
                index = col_t[tile * SUB : (tile + 1) * SUB, :]
                lane = index & (BLK - 1)
                block = index >> (BLK.bit_length() - 1)
                value = jnp.take_along_axis(block_rows[0], lane, axis=1)
                for blk in range(1, per):
                    value = jnp.where(
                        block == blk, jnp.take_along_axis(block_rows[blk], lane, axis=1), value
                    )
                cart[comp, tile * SUB : (tile + 1) * SUB, :] = (
                    value * weight_t[tile * SUB : (tile + 1) * SUB, :]
                )
    number = cycle[0]
    half = lax.rem(number - nside + 1, 2) != 0
    number_f = jnp.full((SUB, LANES), number, jnp.int32).astype(jnp.float32)
    cos_tile = 4.0 / 3.0 - 2.0 * number_f / (3.0 * nside)
    sin_tile = jnp.sqrt(1.0 - cos_tile * cos_tile)
    cos_theta = cos_tile[:1, :]
    sin_theta = sin_tile[:1, :]
    cos_phi, sin_phi = turn_cos[...], turn_sin[...]
    x, y, z = cart[0], cart[1], cart[2]
    east = cos_phi * y - sin_phi * x
    north = sin_theta * z - cos_theta * (cos_phi * x + sin_phi * y)
    samples = jnp.concatenate([east, north], axis=0)
    outer = jnp.concatenate([part("outer_real"), part("outer_imag")], axis=1)
    section = jnp.dot(samples, outer, precision=HIGHEST, preferred_element_type=jnp.float32)
    twist_cos, twist_sin = part("twist_cos"), part("twist_sin")
    turned_real = []
    turned_imag = []
    for f in range(2):
        real = section[f * LANES : (f + 1) * LANES, :LANES]
        imag = section[f * LANES : (f + 1) * LANES, LANES:]
        turned_real.append(real * twist_cos + imag * twist_sin)
        turned_imag.append(imag * twist_cos - real * twist_sin)
    turned = jnp.concatenate(
        [jnp.concatenate(turned_real, axis=1), jnp.concatenate(turned_imag, axis=1)], axis=0
    )
    inner = jnp.concatenate([part("inner_real"), part("inner_imag")], axis=1)
    spectrum = jnp.dot(inner, turned, precision=HIGHEST, preferred_element_type=jnp.float32)
    rows = field.shape[1]
    half_cos, half_sin = part("half_cos"), part("half_sin")
    rot_cos = jnp.where(half, half_cos, half_cos * half_cos - half_sin * half_sin)
    rot_sin = jnp.where(half, half_sin, 2.0 * half_cos * half_sin)
    for f in range(2):
        real = spectrum[:rows, f * LANES : (f + 1) * LANES]
        imag = spectrum[rows:, f * LANES : (f + 1) * LANES]
        field[2 * f] = real * rot_cos + imag * rot_sin
        field[2 * f + 1] = imag * rot_cos - real * rot_sin
    low = lax.broadcasted_iota(jnp.int32, (SUB, LANES), 1) < LANES // 2
    for top in range(0, rows, SUB):
        wave = order[top : top + SUB, :]
        lane = wave & (LANES - 1)
        block = wave >> (LANES.bit_length() - 1)
        picked = []
        for k in range(4):
            value = None
            for blk in range(rows):
                source = jnp.broadcast_to(field[k, blk : blk + 1, :], (SUB, LANES))
                found = jnp.take_along_axis(source, lane, axis=1)
                value = found if value is None else jnp.where(block == blk, found, value)
            picked.append(value.astype(jnp.bfloat16).astype(jnp.float32))
        if paired:
            for h in range(2):
                first_f, second_f = picked[2 * h], picked[2 * h + 1]
                out[top : top + SUB, h, :] = jnp.where(
                    low, first_f, pltpu.roll(second_f, LANES // 2, axis=1)
                )
                out[top : top + SUB, 2 + h, :] = jnp.where(
                    low, pltpu.roll(first_f, LANES // 2, axis=1), second_f
                )
        else:
            for k in range(4):
                out[top : top + SUB, k, :] = picked[k]


def cycle_modes(cycle_ids, received, geometry, components, cycle_length, per, paired, spans):
    col_t, weight_t, turn_cos, turn_sin, _, rest, order, _ = geometry
    rows = order.shape[0]
    vmem = pl.BlockSpec(memory_space=pltpu.VMEM)
    return pl.pallas_call(
        functools.partial(
            modes_kernel, spans=spans, per=per, nside=cycle_length // 4, paired=paired
        ),
        out_shape=jax.ShapeDtypeStruct((rows, 4, LANES), jnp.float32),
        in_specs=[pl.BlockSpec(memory_space=pltpu.SMEM)] + [vmem] * 7,
        out_specs=vmem,
        scratch_shapes=[
            pltpu.VMEM((components, LANES, LANES), jnp.float32),
            pltpu.VMEM((4, rows, LANES), jnp.float32),
        ],
        compiler_params=pltpu.CompilerParams(vmem_limit_bytes=VMEM_ALL - ROOM),
        name="modes",
    )(cycle_ids, received, col_t, weight_t, turn_cos, turn_sin, order, rest)


PARTS = ((-1, 1, -1, 2), (1, 0, -1, 3), (-1, 3, 1, 0), (1, 2, 1, 1))


def legendre_kernel(
    modes, first_wave, early, a_hbm, b_hbm, div_hbm, vort_hbm, table_a, table_b, spread, div, vort,
    in_sems, out_sems, *, levels, cycles, group, split
):
    owned = spread.shape[1]
    width = group * cycles
    groups = owned // group
    degrees = table_a.shape[1]

    def fetch(g, which):
        source, target = ((a_hbm, table_a), (b_hbm, table_b))[which]
        rows = pl.ds(g * width, width)
        return pltpu.make_async_copy(source.at[rows, :], target.at[rows, :], in_sems.at[g, which])

    def flush(g, which):
        source, target = ((div, div_hbm), (vort, vort_hbm))[which]
        rows = pl.ds(g * group, group)
        return pltpu.make_async_copy(
            source.at[:, :, rows, :], target.at[:, :, rows, :], out_sems.at[g, which]
        )

    ready = early.shape[1] // width
    for g in range(ready, groups):
        for which in range(2):
            fetch(g, which).start()
    rows = modes.shape[0]
    row = lax.broadcasted_iota(jnp.int32, (rows, levels * split * width), 0)
    lane = lax.broadcasted_iota(jnp.int32, (rows, levels * split * width), 1)
    same = (lax.rem(row, levels * split) == lax.div(lane, width)) & (
        lax.div(row, levels * split) == lax.rem(lane, cycles)
    )
    pick = jnp.where(same, 1.0, 0.0).astype(jnp.bfloat16)
    turned = jnp.transpose(modes[...]).astype(jnp.bfloat16)
    wide = jnp.dot(turned, pick, preferred_element_type=jnp.float32)
    slot = lax.broadcasted_iota(jnp.int32, (owned, width), 0)
    place = lax.broadcasted_iota(jnp.int32, (owned, width), 1)
    own = lax.rem(slot, group) == lax.div(place, cycles)
    for f in range(4):
        h, i = divmod(f, 4 // split)
        for lev in range(levels):
            start = (lev * split + h) * width
            part = wide[i * owned : (i + 1) * owned, start : start + width]
            spread[f * levels + lev] = jnp.where(own, part, 0.0).astype(jnp.bfloat16)
    chunk = min(256, degrees)
    for g in range(groups):
        base = g * group
        pieces = []
        for sign_a, field_a, sign_b, field_b in PARTS:
            for lev in range(levels):
                left = spread[field_a * levels + lev, base : base + group, :]
                right = spread[field_b * levels + lev, base : base + group, :]
                left = left if sign_a > 0 else -left
                right = right if sign_b > 0 else -right
                pieces.append(jnp.concatenate([left, right], axis=1))
        mix = jnp.concatenate(pieces, axis=0)
        waves = first_wave[base : base + group, :]
        if g >= ready:
            fetch(g, 0).wait()
            fetch(g, 1).wait()
        for start in range(0, degrees, chunk):
            at_rows = slice(g * width, (g + 1) * width)
            lanes = slice(start, start + chunk)
            if g < ready:
                both = jnp.concatenate([early[0, at_rows, lanes], early[1, at_rows, lanes]], axis=0)
            else:
                both = jnp.concatenate([table_a[at_rows, lanes], table_b[at_rows, lanes]], axis=0)
            result = jnp.dot(mix, both, preferred_element_type=jnp.float32)
            for at in range(0, chunk, LANES):
                degree = lax.broadcasted_iota(jnp.int32, (group, LANES), 1) + (start + at)
                upper = degree >= waves
                for part in range(4):
                    target = div if part < 2 else vort
                    for lev in range(levels):
                        top = (part * levels + lev) * group
                        lanes = slice(start + at, start + at + LANES)
                        target[part % 2, lev, base : base + group, lanes] = jnp.where(
                            upper, result[top : top + group, at : at + LANES], 0.0
                        )
        flush(g, 0).start()
        flush(g, 1).start()
    for g in range(groups):
        flush(g, 0).wait()
        flush(g, 1).wait()


def legendre_sums(modes, first_wave, early, flat_a, flat_b, owned, levels, split):
    flat = flat_a.shape
    cycles, degrees = flat[0] // owned, flat[1]
    group = math.gcd(owned, GROUP)
    full = (2, levels, owned, degrees)
    out_shape = jax.ShapeDtypeStruct(full, jnp.float32)
    vmem = pl.BlockSpec(memory_space=pltpu.VMEM)
    hbm = pl.BlockSpec(memory_space=pltpu.HBM)
    return pl.pallas_call(
        functools.partial(
            legendre_kernel, levels=levels, cycles=cycles, group=group, split=split
        ),
        out_shape=(out_shape, out_shape),
        in_specs=[vmem, vmem, vmem, hbm, hbm],
        out_specs=(hbm, hbm),
        scratch_shapes=[
            pltpu.VMEM(flat, jnp.bfloat16),
            pltpu.VMEM(flat, jnp.bfloat16),
            pltpu.VMEM((4 * levels, owned, group * cycles), jnp.bfloat16),
            pltpu.VMEM(full, jnp.float32),
            pltpu.VMEM(full, jnp.float32),
            pltpu.SemaphoreType.DMA((owned // group, 2)),
            pltpu.SemaphoreType.DMA((owned // group, 2)),
        ],
        compiler_params=pltpu.CompilerParams(vmem_limit_bytes=VMEM_ALL - ROOM),
        name="legendre",
    )(modes, first_wave, early, far(flat_a), far(flat_b))


def local(winds, remap_w, remap_col, block_pick, cycle_ids, wave_ids, legendre_a, legendre_b):
    band_count = lax.axis_size("band")
    level_count = lax.axis_size("lev")
    components, levels_dev, column_count = winds.shape
    taps, cycle_count, cycle_length = remap_col.shape
    per = block_pick.shape[1] // band_count
    waves = wave_ids.shape[0]
    devices = band_count * level_count
    owned = waves // devices
    assert levels_dev == 1 and cycle_count == 1
    assert taps * cycle_length == LANES * LANES and band_count % SUB == 0
    blocks = winds.reshape(components, column_count // BLK, BLK)
    outgoing = pick_blocks(block_pick, blocks, band_count, per)
    received = lax.all_to_all(outgoing, "band", split_axis=0, concat_axis=0, tiled=True)
    paired = 2 * owned == LANES
    flat_a = legendre_a.reshape(-1, legendre_a.shape[2])
    flat_b = legendre_b.reshape(-1, legendre_b.shape[2])
    table, spans = tables(cycle_length, taps, waves)
    order = wave_ids.reshape(waves // LANES, LANES)
    geometry = cycle_geometry(
        cycle_ids,
        remap_col.reshape(LANES, LANES),
        remap_w.reshape(LANES, LANES),
        order,
        owned,
        cycle_length,
        jnp.asarray(table),
        spans,
        flat_a,
        flat_b,
    )
    chosen = cycle_modes(
        cycle_ids, received, geometry, components, cycle_length, per, paired, spans
    )
    split = 2 if paired else 1
    if paired:
        parcels = chosen.reshape(devices, split, LANES)
    else:
        parcels = jnp.transpose(
            jnp.transpose(chosen, (1, 0, 2)).reshape(4, devices, owned), (1, 0, 2)
        ).reshape(devices, 1, 4 * owned)
    gathered = lax.all_to_all(parcels, ("band", "lev"), split_axis=0, concat_axis=0, tiled=True)
    modes = gathered.reshape(devices * split, 4 * owned // split)
    return legendre_sums(
        modes, geometry[4], geometry[7], flat_a, flat_b, owned, level_count, split
    )


def solution(mesh):
    placed = (
        P(None, "lev", "band"),
        P(None, "band", None),
        P(None, "band", None),
        P(),
        P("band"),
        P(),
        P(("band", "lev"), None, None),
        P(("band", "lev"), None, None),
    )
    return jax.shard_map(
        local,
        mesh=mesh,
        in_specs=placed,
        out_specs=(P(None, None, ("band", "lev"), None), P(None, None, ("band", "lev"), None)),
        check_vma=False,
    )
```

```python
import functools
import math

import jax
import jax.numpy as jnp
import numpy as np
from jax import lax
from jax.experimental import pallas as pl
from jax.experimental.pallas import tpu as pltpu
from jax.sharding import PartitionSpec as P

BLK = 128
LANES = 128
SUB = 8
GROUP = 16
EARLY = 2
VMEM_ALL = 67043328
ROOM = 24000 * 1024


def far(array):
    return pltpu.with_memory_space_constraint(array, pltpu.HBM)


def pick_kernel(picks, winds, out, *, per):
    band = lax.axis_index("band")
    components = winds.shape[0]

    def one_target(t, carry):
        for c in range(per):
            block = picks[t, band * per + c]
            for comp in range(components):
                place, row = divmod(comp * per + c, out.shape[2])
                out[t, place, pl.ds(row, 1), :] = winds[comp, pl.ds(block, 1), :]
        return carry

    lax.fori_loop(0, out.shape[0], one_target, 0, unroll=out.shape[0] <= 8)


def pick_blocks(block_pick, winds, band_count, per):
    components, blocks, _ = winds.shape
    quad = math.gcd(components * per, 4)
    return pl.pallas_call(
        functools.partial(pick_kernel, per=per),
        out_shape=jax.ShapeDtypeStruct(
            (band_count, components * per // quad, quad, BLK), winds.dtype
        ),
        in_specs=[
            pl.BlockSpec(memory_space=pltpu.SMEM),
            pl.BlockSpec(memory_space=pltpu.VMEM),
        ],
        out_specs=pl.BlockSpec(memory_space=pltpu.VMEM),
        compiler_params=pltpu.CompilerParams(vmem_limit_bytes=VMEM_ALL - ROOM),
        name="pick",
    )(far(block_pick), far(winds))


@functools.lru_cache(maxsize=None)
def tables(cycle_length, taps, waves):
    rows = cycle_length // LANES
    b = np.arange(LANES, dtype=np.int64)
    lane_r = np.arange(taps * rows, dtype=np.int64) % rows
    p = np.arange(LANES, dtype=np.int64)
    u = np.arange(waves // LANES, dtype=np.int64)
    turn = 2.0 * np.pi
    azimuth = turn / cycle_length * (LANES * lane_r[None, :] + b[:, None] + 1)
    outer = turn / rows * (lane_r[:, None] * p[None, :] % rows)
    twist = turn / cycle_length * (b[:, None] * p[None, :] % cycle_length)
    inner = turn * ((LANES * u[:, None] * b[None, :]) % cycle_length) / cycle_length
    half_turn = turn / (2 * cycle_length) * (LANES * u[:, None] + p[None, :])
    f32 = np.float32
    parts = dict(
        cos_phi=np.cos(azimuth),
        sin_phi=np.sin(azimuth),
        outer_real=np.cos(outer),
        outer_imag=-np.sin(outer),
        twist_cos=np.cos(twist),
        twist_sin=np.sin(twist),
        inner_real=np.concatenate([np.cos(inner), -np.sin(inner)], 0),
        inner_imag=np.concatenate([np.sin(inner), np.cos(inner)], 0),
        half_cos=np.cos(half_turn),
        half_sin=np.sin(half_turn),
    )
    spans = {}
    top = 0
    for name, part in parts.items():
        spans[name] = slice(top, top + part.shape[0])
        top += part.shape[0]
    spans["rest"] = slice(spans["outer_real"].start, top)
    return np.concatenate(list(parts.values()), 0).astype(np.float32), spans


def placement(cycles, kinds, group):
    row = np.arange(cycles * kinds)[:, None]
    lane = np.arange(kinds * group * cycles)[None, :]
    same = (row % kinds == lane // (group * cycles)) & (row // kinds == lane % cycles)
    return jnp.asarray(same, jnp.bfloat16)


def early_shape(flat, owned):
    group = math.gcd(owned, GROUP)
    return (2, min(EARLY, owned // group) * group * (flat[0] // owned), flat[1])


def geometry_kernel(
    cycle, col, weight, order, table_hbm, a_hbm, b_hbm, place_hbm, col_t, weight_t, turn_cos, turn_sin,
    first_wave, rest, order_near, early, place, line, sems, *, spans, nside
):
    rows = early.shape[1]
    pieces = 4
    step = rows // pieces
    bulk = [pltpu.make_async_copy(place_hbm, place, sems.at[3])] + [
        pltpu.make_async_copy(
            source.at[pl.ds(i * step, step), :],
            early.at[which, pl.ds(i * step, step), :],
            sems.at[4 + which * pieces + i],
        )
        for i in range(pieces)
        for which, source in enumerate((a_hbm, b_hbm))
    ]
    cos_phi = pltpu.make_async_copy(table_hbm.at[spans["cos_phi"], :], turn_cos, sems.at[0])
    sin_phi = pltpu.make_async_copy(table_hbm.at[spans["sin_phi"], :], turn_sin, sems.at[1])
    other = pltpu.make_async_copy(table_hbm.at[spans["rest"], :], rest, sems.at[2])
    cos_phi.start()
    sin_phi.start()
    other.start()
    for copy in bulk:
        copy.start()
    col_t[...] = jnp.transpose(col[...])
    weight_t[...] = jnp.transpose(weight[...])
    order_near[...] = order[...]
    owned = first_wave.shape[0]
    slot = (lax.axis_index("band") * lax.axis_size("lev") + lax.axis_index("lev")) * owned
    mine = order[pl.ds(lax.div(slot, LANES), 1), :]
    line[...] = jnp.transpose(jnp.broadcast_to(mine, (LANES, LANES)))
    first_wave[...] = line[pl.ds(pl.multiple_of(lax.rem(slot, LANES), SUB), owned), :]
    half = lax.rem(cycle[0] - nside + 1, 2) != 0
    spacing = math.pi / (2.0 * nside)
    shift_cos = jnp.where(half, math.cos(0.5 * spacing), 1.0).astype(jnp.float32)
    shift_sin = jnp.where(half, math.sin(0.5 * spacing), 0.0).astype(jnp.float32)
    cos_phi.wait()
    sin_phi.wait()
    base_cos, base_sin = turn_cos[...], turn_sin[...]
    turn_cos[...] = base_cos * shift_cos + base_sin * shift_sin
    turn_sin[...] = base_sin * shift_cos - base_cos * shift_sin
    other.wait()
    for copy in bulk:
        copy.wait()


def cycle_geometry(
    cycle_ids, col, weight, order, owned, levels, split, cycle_length, table, spans, flat_a, flat_b
):
    cycles = flat_a.shape[0] // owned
    place = placement(cycles, levels * split, math.gcd(owned, GROUP))
    vmem = pl.BlockSpec(memory_space=pltpu.VMEM)
    square = (LANES, LANES)
    rest = spans["rest"].stop - spans["rest"].start
    return pl.pallas_call(
        functools.partial(
            geometry_kernel, spans=spans, nside=cycle_length // 4
        ),
        out_shape=(
            jax.ShapeDtypeStruct(square, jnp.int32),
            jax.ShapeDtypeStruct(square, jnp.float32),
            jax.ShapeDtypeStruct(square, jnp.float32),
            jax.ShapeDtypeStruct(square, jnp.float32),
            jax.ShapeDtypeStruct((owned, LANES), jnp.int32),
            jax.ShapeDtypeStruct((rest, LANES), jnp.float32),
            jax.ShapeDtypeStruct(order.shape, jnp.int32),
            jax.ShapeDtypeStruct(early_shape(flat_a.shape, owned), flat_a.dtype),
            jax.ShapeDtypeStruct(place.shape, place.dtype),
        ),
        in_specs=[pl.BlockSpec(memory_space=pltpu.SMEM), vmem, vmem, vmem]
        + [pl.BlockSpec(memory_space=pltpu.HBM)] * 4,
        out_specs=(vmem,) * 9,
        scratch_shapes=[pltpu.VMEM(square, jnp.int32), pltpu.SemaphoreType.DMA((12,))],
        compiler_params=pltpu.CompilerParams(vmem_limit_bytes=VMEM_ALL - ROOM),
        cost_estimate=pl.CostEstimate(flops=10**7, bytes_accessed=10**7, transcendentals=0),
        name="geometry",
    )(cycle_ids, *[far(x) for x in (col, weight, order, table, flat_a, flat_b, place)])


def halves(value):
    high = value.astype(jnp.bfloat16)
    return high, (value - high.astype(jnp.float32)).astype(jnp.bfloat16)


def product(left, right):
    return jnp.dot(left, right, preferred_element_type=jnp.float32)


def modes_kernel(
    cycle, received, col_t, weight_t, turn_cos, turn_sin, order, table, out, cart, field,
    *, spans, per, nside, paired
):
    band_count, _, quad, _ = received.shape
    components = cart.shape[0]
    tiles = LANES // SUB
    groups = band_count // SUB
    first = spans["rest"].start

    def part(name):
        return table[spans[name].start - first : spans[name].stop - first, :]

    for group in range(groups):
        block_rows = [
            [
                received[(slice(group * SUB, (group + 1) * SUB), *divmod(comp * per + blk, quad))]
                for blk in range(per)
            ]
            for comp in range(components)
        ]
        for tile in range(group, tiles, groups):
            rows = slice(tile * SUB, (tile + 1) * SUB)
            index = col_t[rows, :]
            lane = index & (BLK - 1)
            block = index >> (BLK.bit_length() - 1)
            values = [jnp.take_along_axis(part_rows[0], lane, axis=1) for part_rows in block_rows]
            for blk in range(1, per):
                here = block == blk
                for comp in range(components):
                    found = jnp.take_along_axis(block_rows[comp][blk], lane, axis=1)
                    values[comp] = jnp.where(here, found, values[comp])
            for comp in range(components):
                cart[comp, rows, :] = values[comp] * weight_t[rows, :]
    number = cycle[0]
    half = lax.rem(number - nside + 1, 2) != 0
    number_f = jnp.full((SUB, LANES), number, jnp.int32).astype(jnp.float32)
    cos_tile = 4.0 / 3.0 - 2.0 * number_f / (3.0 * nside)
    sin_tile = jnp.sqrt(1.0 - cos_tile * cos_tile)
    cos_theta = cos_tile[:1, :]
    sin_theta = sin_tile[:1, :]
    cos_phi, sin_phi = turn_cos[...], turn_sin[...]
    x, y, z = cart[0], cart[1], cart[2]
    east = cos_phi * y - sin_phi * x
    north = sin_theta * z - cos_theta * (cos_phi * x + sin_phi * y)
    samples = jnp.concatenate([east, north], axis=0)
    outer = jnp.concatenate([part("outer_real"), part("outer_imag")], axis=1)
    outer_high, outer_low = halves(outer)
    high, low = halves(samples)
    section = product(
        jnp.concatenate([high, low, high], axis=1),
        jnp.concatenate([outer_high, outer_high, outer_low], axis=0),
    )
    twist_cos, twist_sin = part("twist_cos"), part("twist_sin")
    turned_real = []
    turned_imag = []
    for f in range(2):
        real = section[f * LANES : (f + 1) * LANES, :LANES]
        imag = section[f * LANES : (f + 1) * LANES, LANES:]
        turned_real.append(real * twist_cos + imag * twist_sin)
        turned_imag.append(imag * twist_cos - real * twist_sin)
    turned = jnp.concatenate(
        [jnp.concatenate(turned_real, axis=1), jnp.concatenate(turned_imag, axis=1)], axis=0
    )
    inner = jnp.concatenate([part("inner_real"), part("inner_imag")], axis=1)
    rows = field.shape[1]
    inner_high, inner_low = halves(inner)
    high, low = halves(turned)
    both = product(jnp.concatenate([inner_high, inner_low], axis=0), high)
    spectrum = both[: 2 * rows] + both[2 * rows :] + product(inner_high, low)
    half_cos, half_sin = part("half_cos"), part("half_sin")
    rot_cos = jnp.where(half, half_cos, half_cos * half_cos - half_sin * half_sin)
    rot_sin = jnp.where(half, half_sin, 2.0 * half_cos * half_sin)
    for f in range(2):
        real = spectrum[:rows, f * LANES : (f + 1) * LANES]
        imag = spectrum[rows:, f * LANES : (f + 1) * LANES]
        field[2 * f] = real * rot_cos + imag * rot_sin
        field[2 * f + 1] = imag * rot_cos - real * rot_sin
    front = lax.broadcasted_iota(jnp.int32, (SUB, LANES), 1) < LANES // 2
    for top in range(0, rows, SUB):
        wave = order[top : top + SUB, :]
        lane = wave & (LANES - 1)
        block = wave >> (LANES.bit_length() - 1)
        picked = []
        for k in range(4):
            value = None
            for blk in range(rows):
                source = jnp.broadcast_to(field[k, blk : blk + 1, :], (SUB, LANES))
                found = jnp.take_along_axis(source, lane, axis=1)
                value = found if value is None else jnp.where(block == blk, found, value)
            picked.append(value.astype(jnp.bfloat16).astype(jnp.float32))
        if paired:
            for h in range(2):
                first_f, second_f = picked[2 * h], picked[2 * h + 1]
                out[top : top + SUB, h, :] = jnp.where(
                    front, first_f, pltpu.roll(second_f, LANES // 2, axis=1)
                )
                out[top : top + SUB, 2 + h, :] = jnp.where(
                    front, pltpu.roll(first_f, LANES // 2, axis=1), second_f
                )
        else:
            for k in range(4):
                out[top : top + SUB, k, :] = picked[k]


def cycle_modes(cycle_ids, received, geometry, components, cycle_length, per, paired, spans):
    col_t, weight_t, turn_cos, turn_sin, _, rest, order, _, _ = geometry
    rows = order.shape[0]
    vmem = pl.BlockSpec(memory_space=pltpu.VMEM)
    return pl.pallas_call(
        functools.partial(
            modes_kernel, spans=spans, per=per, nside=cycle_length // 4, paired=paired
        ),
        out_shape=jax.ShapeDtypeStruct((rows, 4, LANES), jnp.float32),
        in_specs=[pl.BlockSpec(memory_space=pltpu.SMEM)] + [vmem] * 7,
        out_specs=vmem,
        scratch_shapes=[
            pltpu.VMEM((components, LANES, LANES), jnp.float32),
            pltpu.VMEM((4, rows, LANES), jnp.float32),
        ],
        compiler_params=pltpu.CompilerParams(vmem_limit_bytes=VMEM_ALL - ROOM),
        name="modes",
    )(cycle_ids, received, col_t, weight_t, turn_cos, turn_sin, order, rest)


PARTS = ((-1, 1, -1, 2), (1, 0, -1, 3), (-1, 3, 1, 0), (1, 2, 1, 1))


def legendre_kernel(
    modes, first_wave, early, place, a_hbm, b_hbm, div_hbm, vort_hbm, table_a, table_b, turned, div, vort,
    in_sems, out_sems, *, levels, cycles, group, split
):
    owned = turned.shape[0] * split // 4
    width = group * cycles
    groups = owned // group
    degrees = table_a.shape[1]

    def fetch(g, which):
        source, target = ((a_hbm, table_a), (b_hbm, table_b))[which]
        rows = pl.ds(g * width, width)
        return pltpu.make_async_copy(source.at[rows, :], target.at[rows, :], in_sems.at[g, which])

    def flush(g, which):
        source, target = ((div, div_hbm), (vort, vort_hbm))[which]
        rows = pl.ds(g * group, group)
        return pltpu.make_async_copy(
            source.at[:, :, rows, :], target.at[:, :, rows, :], out_sems.at[g, which]
        )

    ready = early.shape[1] // width
    for g in range(ready, groups):
        for which in range(2):
            fetch(g, which).start()
    turned[...] = jnp.transpose(modes[...])
    slot = lax.broadcasted_iota(jnp.int32, (group, width), 0)
    entry = lax.broadcasted_iota(jnp.int32, (group, width), 1)
    own = slot == lax.div(entry, cycles)
    fields = 4 // split
    chunk = min(256, degrees)
    for g in range(groups):
        base = g * group
        mine = jnp.concatenate(
            [turned[i * owned + base : i * owned + base + group, :] for i in range(fields)], axis=0
        ).astype(jnp.bfloat16)
        wide = jnp.dot(mine, place[...], preferred_element_type=jnp.float32)

        def spread(f, lev, sign):
            h, i = divmod(f, fields)
            start = (lev * split + h) * width
            part = wide[i * group : (i + 1) * group, start : start + width]
            return jnp.where(own, part if sign > 0 else -part, 0.0)

        mix = jnp.concatenate(
            [
                jnp.concatenate(
                    [spread(field_a, lev, sign_a), spread(field_b, lev, sign_b)], axis=1
                )
                for sign_a, field_a, sign_b, field_b in PARTS
                for lev in range(levels)
            ],
            axis=0,
        ).astype(jnp.bfloat16)
        waves = first_wave[base : base + group, :]
        if g >= ready:
            fetch(g, 0).wait()
            fetch(g, 1).wait()
        for start in range(0, degrees, chunk):
            at_rows = slice(g * width, (g + 1) * width)
            lanes = slice(start, start + chunk)
            if g < ready:
                both = jnp.concatenate([early[0, at_rows, lanes], early[1, at_rows, lanes]], axis=0)
            else:
                both = jnp.concatenate([table_a[at_rows, lanes], table_b[at_rows, lanes]], axis=0)
            result = jnp.dot(mix, both, preferred_element_type=jnp.float32)
            for at in range(0, chunk, LANES):
                degree = lax.broadcasted_iota(jnp.int32, (group, LANES), 1) + (start + at)
                upper = degree >= waves
                for part in range(4):
                    target = div if part < 2 else vort
                    for lev in range(levels):
                        top = (part * levels + lev) * group
                        lanes = slice(start + at, start + at + LANES)
                        target[part % 2, lev, base : base + group, lanes] = jnp.where(
                            upper, result[top : top + group, at : at + LANES], 0.0
                        )
        flush(g, 0).start()
        flush(g, 1).start()
    for g in range(groups):
        flush(g, 0).wait()
        flush(g, 1).wait()


def legendre_sums(modes, first_wave, early, place, flat_a, flat_b, owned, levels, split):
    flat = flat_a.shape
    cycles, degrees = flat[0] // owned, flat[1]
    group = math.gcd(owned, GROUP)
    full = (2, levels, owned, degrees)
    out_shape = jax.ShapeDtypeStruct(full, jnp.float32)
    vmem = pl.BlockSpec(memory_space=pltpu.VMEM)
    hbm = pl.BlockSpec(memory_space=pltpu.HBM)
    return pl.pallas_call(
        functools.partial(
            legendre_kernel, levels=levels, cycles=cycles, group=group, split=split
        ),
        out_shape=(out_shape, out_shape),
        in_specs=[vmem, vmem, vmem, vmem, hbm, hbm],
        out_specs=(hbm, hbm),
        scratch_shapes=[
            pltpu.VMEM(flat, jnp.bfloat16),
            pltpu.VMEM(flat, jnp.bfloat16),
            pltpu.VMEM(modes.shape[::-1], jnp.float32),
            pltpu.VMEM(full, jnp.float32),
            pltpu.VMEM(full, jnp.float32),
            pltpu.SemaphoreType.DMA((owned // group, 2)),
            pltpu.SemaphoreType.DMA((owned // group, 2)),
        ],
        compiler_params=pltpu.CompilerParams(vmem_limit_bytes=VMEM_ALL - ROOM),
        name="legendre",
    )(modes, first_wave, early, place, far(flat_a), far(flat_b))


def local(winds, remap_w, remap_col, block_pick, cycle_ids, wave_ids, legendre_a, legendre_b):
    band_count = lax.axis_size("band")
    level_count = lax.axis_size("lev")
    components, levels_dev, column_count = winds.shape
    taps, cycle_count, cycle_length = remap_col.shape
    per = block_pick.shape[1] // band_count
    waves = wave_ids.shape[0]
    devices = band_count * level_count
    owned = waves // devices
    assert levels_dev == 1 and cycle_count == 1
    assert taps * cycle_length == LANES * LANES and band_count % SUB == 0
    blocks = winds.reshape(components, column_count // BLK, BLK)
    outgoing = pick_blocks(block_pick, blocks, band_count, per)
    received = lax.all_to_all(outgoing, "band", split_axis=0, concat_axis=0, tiled=True)
    paired = 2 * owned == LANES
    split = 2 if paired else 1
    flat_a = legendre_a.reshape(-1, legendre_a.shape[2])
    flat_b = legendre_b.reshape(-1, legendre_b.shape[2])
    table, spans = tables(cycle_length, taps, waves)
    order = wave_ids.reshape(waves // LANES, LANES)
    geometry = cycle_geometry(
        cycle_ids,
        remap_col.reshape(LANES, LANES),
        remap_w.reshape(LANES, LANES),
        order,
        owned,
        level_count,
        split,
        cycle_length,
        jnp.asarray(table),
        spans,
        flat_a,
        flat_b,
    )
    chosen = cycle_modes(
        cycle_ids, received, geometry, components, cycle_length, per, paired, spans
    )
    if paired:
        parcels = chosen.reshape(devices, split, LANES)
    else:
        parcels = jnp.transpose(
            jnp.transpose(chosen, (1, 0, 2)).reshape(4, devices, owned), (1, 0, 2)
        ).reshape(devices, 1, 4 * owned)
    gathered = lax.all_to_all(parcels, ("band", "lev"), split_axis=0, concat_axis=0, tiled=True)
    modes = gathered.reshape(devices * split, 4 * owned // split)
    return legendre_sums(
        modes, geometry[4], geometry[7], geometry[8], flat_a, flat_b, owned, level_count, split
    )


def solution(mesh):
    placed = (
        P(None, "lev", "band"),
        P(None, "band", None),
        P(None, "band", None),
        P(),
        P("band"),
        P(),
        P(("band", "lev"), None, None),
        P(("band", "lev"), None, None),
    )
    return jax.shard_map(
        local,
        mesh=mesh,
        in_specs=placed,
        out_specs=(P(None, None, ("band", "lev"), None), P(None, None, ("band", "lev"), None)),
        check_vma=False,
    )
```

```python
import functools
import math

import jax
import jax.numpy as jnp
import numpy as np
from jax import lax
from jax.experimental import pallas as pl
from jax.experimental.pallas import tpu as pltpu
from jax.sharding import PartitionSpec as P

BLK = 128
LANES = 128
SUB = 8
GROUP = 16
EARLY = 2
VMEM_ALL = 67043328
ROOM = 24000 * 1024


def far(array):
    return pltpu.with_memory_space_constraint(array, pltpu.HBM)


def pick_kernel(picks, winds, out, *, per):
    band = lax.axis_index("band")
    components = winds.shape[0]

    def one_target(t, carry):
        for c in range(per):
            block = picks[t, band * per + c]
            for comp in range(components):
                place, row = divmod(comp * per + c, out.shape[2])
                out[t, place, pl.ds(row, 1), :] = winds[comp, pl.ds(block, 1), :]
        return carry

    lax.fori_loop(0, out.shape[0], one_target, 0, unroll=out.shape[0] <= 8)


def pick_blocks(block_pick, winds, band_count, per):
    components, blocks, _ = winds.shape
    quad = math.gcd(components * per, 4)
    return pl.pallas_call(
        functools.partial(pick_kernel, per=per),
        out_shape=jax.ShapeDtypeStruct(
            (band_count, components * per // quad, quad, BLK), winds.dtype
        ),
        in_specs=[
            pl.BlockSpec(memory_space=pltpu.SMEM),
            pl.BlockSpec(memory_space=pltpu.VMEM),
        ],
        out_specs=pl.BlockSpec(memory_space=pltpu.VMEM),
        compiler_params=pltpu.CompilerParams(vmem_limit_bytes=VMEM_ALL - ROOM),
        name="pick",
    )(far(block_pick), far(winds))


@functools.lru_cache(maxsize=None)
def tables(cycle_length, taps, waves):
    rows = cycle_length // LANES
    b = np.arange(LANES, dtype=np.int64)
    lane_r = np.arange(taps * rows, dtype=np.int64) % rows
    p = np.arange(LANES, dtype=np.int64)
    u = np.arange(waves // LANES, dtype=np.int64)
    turn = 2.0 * np.pi
    azimuth = turn / cycle_length * (LANES * lane_r[None, :] + b[:, None] + 1)
    outer = turn / rows * (lane_r[:, None] * p[None, :] % rows)
    twist = turn / cycle_length * (b[:, None] * p[None, :] % cycle_length)
    inner = turn * ((LANES * u[:, None] * b[None, :]) % cycle_length) / cycle_length
    half_turn = turn / (2 * cycle_length) * (LANES * u[:, None] + p[None, :])
    f32 = np.float32
    parts = dict(
        cos_phi=np.cos(azimuth),
        sin_phi=np.sin(azimuth),
        outer_real=np.cos(outer),
        outer_imag=-np.sin(outer),
        twist_cos=np.cos(twist),
        twist_sin=np.sin(twist),
        inner_real=np.concatenate([np.cos(inner), -np.sin(inner)], 0),
        inner_imag=np.concatenate([np.sin(inner), np.cos(inner)], 0),
        half_cos=np.cos(half_turn),
        half_sin=np.sin(half_turn),
    )
    spans = {}
    top = 0
    for name, part in parts.items():
        spans[name] = slice(top, top + part.shape[0])
        top += part.shape[0]
    spans["rest"] = slice(spans["outer_real"].start, top)
    return np.concatenate(list(parts.values()), 0).astype(np.float32), spans


def placement(cycles, kinds, group):
    row = np.arange(cycles * kinds)[:, None]
    lane = np.arange(kinds * group * cycles)[None, :]
    same = (row % kinds == lane // (group * cycles)) & (row // kinds == lane % cycles)
    return jnp.asarray(same, jnp.bfloat16)


def early_shape(flat, owned):
    group = math.gcd(owned, GROUP)
    return (2, min(EARLY, owned // group) * group * (flat[0] // owned), flat[1])


def geometry_kernel(
    cycle, col, weight, order, table_hbm, a_hbm, b_hbm, place_hbm, col_t, weight_t, turn_cos, turn_sin,
    first_wave, rest, order_near, early, place, line, sems, *, spans, nside
):
    rows = early.shape[1]
    pieces = 4
    step = rows // pieces
    bulk = [pltpu.make_async_copy(place_hbm, place, sems.at[3])] + [
        pltpu.make_async_copy(
            source.at[pl.ds(i * step, step), :],
            early.at[which, pl.ds(i * step, step), :],
            sems.at[4 + which * pieces + i],
        )
        for i in range(pieces)
        for which, source in enumerate((a_hbm, b_hbm))
    ]
    cos_phi = pltpu.make_async_copy(table_hbm.at[spans["cos_phi"], :], turn_cos, sems.at[0])
    sin_phi = pltpu.make_async_copy(table_hbm.at[spans["sin_phi"], :], turn_sin, sems.at[1])
    other = pltpu.make_async_copy(table_hbm.at[spans["rest"], :], rest, sems.at[2])
    cos_phi.start()
    sin_phi.start()
    other.start()
    for copy in bulk:
        copy.start()
    col_t[...] = jnp.transpose(col[...])
    weight_t[...] = jnp.transpose(weight[...])
    order_near[...] = order[...]
    owned = first_wave.shape[0]
    slot = (lax.axis_index("band") * lax.axis_size("lev") + lax.axis_index("lev")) * owned
    mine = order[pl.ds(lax.div(slot, LANES), 1), :]
    line[...] = jnp.transpose(jnp.broadcast_to(mine, (LANES, LANES)))
    first_wave[...] = line[pl.ds(pl.multiple_of(lax.rem(slot, LANES), SUB), owned), :]
    half = lax.rem(cycle[0] - nside + 1, 2) != 0
    spacing = math.pi / (2.0 * nside)
    shift_cos = jnp.where(half, math.cos(0.5 * spacing), 1.0).astype(jnp.float32)
    shift_sin = jnp.where(half, math.sin(0.5 * spacing), 0.0).astype(jnp.float32)
    cos_phi.wait()
    sin_phi.wait()
    base_cos, base_sin = turn_cos[...], turn_sin[...]
    turn_cos[...] = base_cos * shift_cos + base_sin * shift_sin
    turn_sin[...] = base_sin * shift_cos - base_cos * shift_sin
    other.wait()
    for copy in bulk:
        copy.wait()


def cycle_geometry(
    cycle_ids, col, weight, order, owned, levels, split, cycle_length, table, spans, flat_a, flat_b
):
    cycles = flat_a.shape[0] // owned
    place = placement(cycles, levels * split, math.gcd(owned, GROUP))
    vmem = pl.BlockSpec(memory_space=pltpu.VMEM)
    square = (LANES, LANES)
    rest = spans["rest"].stop - spans["rest"].start
    return pl.pallas_call(
        functools.partial(
            geometry_kernel, spans=spans, nside=cycle_length // 4
        ),
        out_shape=(
            jax.ShapeDtypeStruct(square, jnp.int32),
            jax.ShapeDtypeStruct(square, jnp.float32),
            jax.ShapeDtypeStruct(square, jnp.float32),
            jax.ShapeDtypeStruct(square, jnp.float32),
            jax.ShapeDtypeStruct((owned, LANES), jnp.int32),
            jax.ShapeDtypeStruct((rest, LANES), jnp.float32),
            jax.ShapeDtypeStruct(order.shape, jnp.int32),
            jax.ShapeDtypeStruct(early_shape(flat_a.shape, owned), flat_a.dtype),
            jax.ShapeDtypeStruct(place.shape, place.dtype),
        ),
        in_specs=[pl.BlockSpec(memory_space=pltpu.SMEM), vmem, vmem, vmem]
        + [pl.BlockSpec(memory_space=pltpu.HBM)] * 4,
        out_specs=(vmem,) * 9,
        scratch_shapes=[pltpu.VMEM(square, jnp.int32), pltpu.SemaphoreType.DMA((12,))],
        compiler_params=pltpu.CompilerParams(vmem_limit_bytes=VMEM_ALL - ROOM),
        cost_estimate=pl.CostEstimate(flops=10**7, bytes_accessed=10**7, transcendentals=0),
        name="geometry",
    )(cycle_ids, *[far(x) for x in (col, weight, order, table, flat_a, flat_b, place)])


def halves(value):
    high = value.astype(jnp.bfloat16)
    return high, (value - high.astype(jnp.float32)).astype(jnp.bfloat16)


def product(left, right):
    return jnp.dot(left, right, preferred_element_type=jnp.float32)


def modes_kernel(
    cycle, received, col_t, weight_t, turn_cos, turn_sin, order, table, out, cart, field,
    *, spans, per, nside, paired
):
    components = cart.shape[0]
    span = components * per
    band_count = received.shape[0] // span
    tiles = LANES // SUB
    groups = band_count // SUB
    first = spans["rest"].start

    def part(name):
        return table[spans[name].start - first : spans[name].stop - first, :]

    for group in range(groups):
        block_rows = [
            [
                received[pl.ds(group * SUB * span + comp * per + blk, SUB, stride=span), :]
                for blk in range(per)
            ]
            for comp in range(components)
        ]
        for tile in range(group, tiles, groups):
            rows = slice(tile * SUB, (tile + 1) * SUB)
            index = col_t[rows, :]
            lane = index & (BLK - 1)
            block = index >> (BLK.bit_length() - 1)
            values = [jnp.take_along_axis(part_rows[0], lane, axis=1) for part_rows in block_rows]
            for blk in range(1, per):
                here = block == blk
                for comp in range(components):
                    found = jnp.take_along_axis(block_rows[comp][blk], lane, axis=1)
                    values[comp] = jnp.where(here, found, values[comp])
            for comp in range(components):
                cart[comp, rows, :] = values[comp] * weight_t[rows, :]
    number = cycle[0]
    half = lax.rem(number - nside + 1, 2) != 0
    number_f = jnp.full((SUB, LANES), number, jnp.int32).astype(jnp.float32)
    cos_tile = 4.0 / 3.0 - 2.0 * number_f / (3.0 * nside)
    sin_tile = jnp.sqrt(1.0 - cos_tile * cos_tile)
    cos_theta = cos_tile[:1, :]
    sin_theta = sin_tile[:1, :]
    cos_phi, sin_phi = turn_cos[...], turn_sin[...]
    x, y, z = cart[0], cart[1], cart[2]
    east = cos_phi * y - sin_phi * x
    north = sin_theta * z - cos_theta * (cos_phi * x + sin_phi * y)
    samples = jnp.concatenate([east, north], axis=0)
    outer = jnp.concatenate([part("outer_real"), part("outer_imag")], axis=1)
    outer_high, outer_low = halves(outer)
    high, low = halves(samples)
    section = product(
        jnp.concatenate([high, low, high], axis=1),
        jnp.concatenate([outer_high, outer_high, outer_low], axis=0),
    )
    twist_cos, twist_sin = part("twist_cos"), part("twist_sin")
    turned_real = []
    turned_imag = []
    for f in range(2):
        real = section[f * LANES : (f + 1) * LANES, :LANES]
        imag = section[f * LANES : (f + 1) * LANES, LANES:]
        turned_real.append(real * twist_cos + imag * twist_sin)
        turned_imag.append(imag * twist_cos - real * twist_sin)
    turned = jnp.concatenate(
        [jnp.concatenate(turned_real, axis=1), jnp.concatenate(turned_imag, axis=1)], axis=0
    )
    inner = jnp.concatenate([part("inner_real"), part("inner_imag")], axis=1)
    rows = field.shape[1]
    inner_high, inner_low = halves(inner)
    high, low = halves(turned)
    both = product(jnp.concatenate([inner_high, inner_low], axis=0), high)
    spectrum = both[: 2 * rows] + both[2 * rows :] + product(inner_high, low)
    half_cos, half_sin = part("half_cos"), part("half_sin")
    rot_cos = jnp.where(half, half_cos, half_cos * half_cos - half_sin * half_sin)
    rot_sin = jnp.where(half, half_sin, 2.0 * half_cos * half_sin)
    for f in range(2):
        real = spectrum[:rows, f * LANES : (f + 1) * LANES]
        imag = spectrum[rows:, f * LANES : (f + 1) * LANES]
        field[2 * f] = real * rot_cos + imag * rot_sin
        field[2 * f + 1] = imag * rot_cos - real * rot_sin
    front = lax.broadcasted_iota(jnp.int32, (SUB, LANES), 1) < LANES // 2
    for top in range(0, rows, SUB):
        wave = order[top : top + SUB, :]
        lane = wave & (LANES - 1)
        block = wave >> (LANES.bit_length() - 1)
        picked = []
        for k in range(4):
            value = None
            for blk in range(rows):
                source = jnp.broadcast_to(field[k, blk : blk + 1, :], (SUB, LANES))
                found = jnp.take_along_axis(source, lane, axis=1)
                value = found if value is None else jnp.where(block == blk, found, value)
            picked.append(value.astype(jnp.bfloat16).astype(jnp.float32))
        if paired:
            for h in range(2):
                first_f, second_f = picked[2 * h], picked[2 * h + 1]
                out[top : top + SUB, h, :] = jnp.where(
                    front, first_f, pltpu.roll(second_f, LANES // 2, axis=1)
                )
                out[top : top + SUB, 2 + h, :] = jnp.where(
                    front, pltpu.roll(first_f, LANES // 2, axis=1), second_f
                )
        else:
            for k in range(4):
                out[top : top + SUB, k, :] = picked[k]


def cycle_modes(cycle_ids, received, geometry, components, cycle_length, per, paired, spans):
    col_t, weight_t, turn_cos, turn_sin, _, rest, order, _, _ = geometry
    rows = order.shape[0]
    vmem = pl.BlockSpec(memory_space=pltpu.VMEM)
    return pl.pallas_call(
        functools.partial(
            modes_kernel, spans=spans, per=per, nside=cycle_length // 4, paired=paired
        ),
        out_shape=jax.ShapeDtypeStruct((rows, 4, LANES), jnp.float32),
        in_specs=[pl.BlockSpec(memory_space=pltpu.SMEM)] + [vmem] * 7,
        out_specs=vmem,
        scratch_shapes=[
            pltpu.VMEM((components, LANES, LANES), jnp.float32),
            pltpu.VMEM((4, rows, LANES), jnp.float32),
        ],
        compiler_params=pltpu.CompilerParams(vmem_limit_bytes=VMEM_ALL - ROOM),
        name="modes",
    )(cycle_ids, received, col_t, weight_t, turn_cos, turn_sin, order, rest)


PARTS = ((-1, 1, -1, 2), (1, 0, -1, 3), (-1, 3, 1, 0), (1, 2, 1, 1))


def legendre_kernel(
    modes, first_wave, early, place, a_hbm, b_hbm, div_hbm, vort_hbm, table_a, table_b, turned, div, vort,
    in_sems, out_sems, *, levels, cycles, group, split
):
    owned = turned.shape[0] * split // 4
    width = group * cycles
    groups = owned // group
    degrees = table_a.shape[1]

    def fetch(g, which):
        source, target = ((a_hbm, table_a), (b_hbm, table_b))[which]
        rows = pl.ds(g * width, width)
        return pltpu.make_async_copy(source.at[rows, :], target.at[rows, :], in_sems.at[g, which])

    def flush(g, which):
        source, target = ((div, div_hbm), (vort, vort_hbm))[which]
        rows = pl.ds(g * group, group)
        return pltpu.make_async_copy(
            source.at[:, :, rows, :], target.at[:, :, rows, :], out_sems.at[g, which]
        )

    ready = early.shape[1] // width
    for g in range(ready, groups):
        for which in range(2):
            fetch(g, which).start()
    turned[...] = jnp.transpose(modes[...])
    slot = lax.broadcasted_iota(jnp.int32, (group, width), 0)
    entry = lax.broadcasted_iota(jnp.int32, (group, width), 1)
    own = slot == lax.div(entry, cycles)
    fields = 4 // split
    chunk = min(256, degrees)
    for g in range(groups):
        base = g * group
        mine = jnp.concatenate(
            [turned[i * owned + base : i * owned + base + group, :] for i in range(fields)], axis=0
        ).astype(jnp.bfloat16)
        wide = jnp.dot(mine, place[...], preferred_element_type=jnp.float32)

        def spread(f, lev, sign):
            h, i = divmod(f, fields)
            start = (lev * split + h) * width
            part = wide[i * group : (i + 1) * group, start : start + width]
            return jnp.where(own, part if sign > 0 else -part, 0.0)

        mix = jnp.concatenate(
            [
                jnp.concatenate(
                    [spread(field_a, lev, sign_a), spread(field_b, lev, sign_b)], axis=1
                )
                for sign_a, field_a, sign_b, field_b in PARTS
                for lev in range(levels)
            ],
            axis=0,
        ).astype(jnp.bfloat16)
        waves = first_wave[base : base + group, :]
        if g >= ready:
            fetch(g, 0).wait()
            fetch(g, 1).wait()
        for start in range(0, degrees, chunk):
            at_rows = slice(g * width, (g + 1) * width)
            lanes = slice(start, start + chunk)
            if g < ready:
                both = jnp.concatenate([early[0, at_rows, lanes], early[1, at_rows, lanes]], axis=0)
            else:
                both = jnp.concatenate([table_a[at_rows, lanes], table_b[at_rows, lanes]], axis=0)
            result = jnp.dot(mix, both, preferred_element_type=jnp.float32)
            for at in range(0, chunk, LANES):
                degree = lax.broadcasted_iota(jnp.int32, (group, LANES), 1) + (start + at)
                upper = degree >= waves
                for part in range(4):
                    target = div if part < 2 else vort
                    for lev in range(levels):
                        top = (part * levels + lev) * group
                        lanes = slice(start + at, start + at + LANES)
                        target[part % 2, lev, base : base + group, lanes] = jnp.where(
                            upper, result[top : top + group, at : at + LANES], 0.0
                        )
        flush(g, 0).start()
        flush(g, 1).start()
    for g in range(groups):
        flush(g, 0).wait()
        flush(g, 1).wait()


def legendre_sums(modes, first_wave, early, place, flat_a, flat_b, owned, levels, split):
    flat = flat_a.shape
    cycles, degrees = flat[0] // owned, flat[1]
    group = math.gcd(owned, GROUP)
    full = (2, levels, owned, degrees)
    out_shape = jax.ShapeDtypeStruct(full, jnp.float32)
    vmem = pl.BlockSpec(memory_space=pltpu.VMEM)
    hbm = pl.BlockSpec(memory_space=pltpu.HBM)
    return pl.pallas_call(
        functools.partial(
            legendre_kernel, levels=levels, cycles=cycles, group=group, split=split
        ),
        out_shape=(out_shape, out_shape),
        in_specs=[vmem, vmem, vmem, vmem, hbm, hbm],
        out_specs=(hbm, hbm),
        scratch_shapes=[
            pltpu.VMEM(flat, jnp.bfloat16),
            pltpu.VMEM(flat, jnp.bfloat16),
            pltpu.VMEM(modes.shape[::-1], jnp.float32),
            pltpu.VMEM(full, jnp.float32),
            pltpu.VMEM(full, jnp.float32),
            pltpu.SemaphoreType.DMA((owned // group, 2)),
            pltpu.SemaphoreType.DMA((owned // group, 2)),
        ],
        compiler_params=pltpu.CompilerParams(vmem_limit_bytes=VMEM_ALL - ROOM),
        name="legendre",
    )(modes, first_wave, early, place, far(flat_a), far(flat_b))


def local(winds, remap_w, remap_col, block_pick, cycle_ids, wave_ids, legendre_a, legendre_b):
    band_count = lax.axis_size("band")
    level_count = lax.axis_size("lev")
    components, levels_dev, column_count = winds.shape
    taps, cycle_count, cycle_length = remap_col.shape
    per = block_pick.shape[1] // band_count
    waves = wave_ids.shape[0]
    devices = band_count * level_count
    owned = waves // devices
    assert levels_dev == 1 and cycle_count == 1
    assert taps * cycle_length == LANES * LANES and band_count % SUB == 0
    blocks = winds.reshape(components, column_count // BLK, BLK)
    outgoing = pick_blocks(block_pick, blocks, band_count, per)
    received = lax.all_to_all(outgoing, "band", split_axis=0, concat_axis=0, tiled=True)
    received = received.reshape(band_count * components * per, BLK)
    paired = 2 * owned == LANES
    split = 2 if paired else 1
    flat_a = legendre_a.reshape(-1, legendre_a.shape[2])
    flat_b = legendre_b.reshape(-1, legendre_b.shape[2])
    table, spans = tables(cycle_length, taps, waves)
    order = wave_ids.reshape(waves // LANES, LANES)
    geometry = cycle_geometry(
        cycle_ids,
        remap_col.reshape(LANES, LANES),
        remap_w.reshape(LANES, LANES),
        order,
        owned,
        level_count,
        split,
        cycle_length,
        jnp.asarray(table),
        spans,
        flat_a,
        flat_b,
    )
    chosen = cycle_modes(
        cycle_ids, received, geometry, components, cycle_length, per, paired, spans
    )
    if paired:
        parcels = chosen.reshape(devices, split, LANES)
    else:
        parcels = jnp.transpose(
            jnp.transpose(chosen.reshape(-1, 4, LANES), (1, 0, 2)).reshape(4, devices, owned), (1, 0, 2)
        ).reshape(devices, 1, 4 * owned)
    gathered = lax.all_to_all(parcels, ("band", "lev"), split_axis=0, concat_axis=0, tiled=True)
    modes = gathered.reshape(devices * split, 4 * owned // split)
    return legendre_sums(
        modes, geometry[4], geometry[7], geometry[8], flat_a, flat_b, owned, level_count, split
    )


def solution(mesh):
    placed = (
        P(None, "lev", "band"),
        P(None, "band", None),
        P(None, "band", None),
        P(),
        P("band"),
        P(),
        P(("band", "lev"), None, None),
        P(("band", "lev"), None, None),
    )
    return jax.shard_map(
        local,
        mesh=mesh,
        in_specs=placed,
        out_specs=(P(None, None, ("band", "lev"), None), P(None, None, ("band", "lev"), None)),
        check_vma=False,
    )
```

```python
import functools
import math

import jax
import jax.numpy as jnp
import numpy as np
from jax import lax
from jax.experimental import pallas as pl
from jax.experimental.pallas import tpu as pltpu
from jax.sharding import PartitionSpec as P

BLK = 128
LANES = 128
SUB = 8
GROUP = 16
EARLY = 2
VMEM_ALL = 67043328
ROOM = 24000 * 1024


def far(array):
    return pltpu.with_memory_space_constraint(array, pltpu.HBM)


def pick_kernel(picks, winds, out, *, per):
    band = lax.axis_index("band")
    components = winds.shape[0]

    def one_target(t, carry):
        for c in range(per):
            block = picks[t, band * per + c]
            for comp in range(components):
                place, row = divmod(comp * per + c, out.shape[2])
                out[t, place, pl.ds(row, 1), :] = winds[comp, pl.ds(block, 1), :]
        return carry

    lax.fori_loop(0, out.shape[0], one_target, 0, unroll=out.shape[0] <= 8)


def pick_blocks(block_pick, winds, band_count, per):
    components, blocks, _ = winds.shape
    quad = math.gcd(components * per, 4)
    return pl.pallas_call(
        functools.partial(pick_kernel, per=per),
        out_shape=jax.ShapeDtypeStruct(
            (band_count, components * per // quad, quad, BLK), winds.dtype
        ),
        in_specs=[
            pl.BlockSpec(memory_space=pltpu.SMEM),
            pl.BlockSpec(memory_space=pltpu.VMEM),
        ],
        out_specs=pl.BlockSpec(memory_space=pltpu.VMEM),
        compiler_params=pltpu.CompilerParams(vmem_limit_bytes=VMEM_ALL - ROOM),
        name="pick",
    )(far(block_pick), far(winds))


@functools.lru_cache(maxsize=None)
def tables(cycle_length, taps, waves):
    rows = cycle_length // LANES
    b = np.arange(LANES, dtype=np.int64)
    lane_r = np.arange(taps * rows, dtype=np.int64) % rows
    p = np.arange(LANES, dtype=np.int64)
    u = np.arange(waves // LANES, dtype=np.int64)
    turn = 2.0 * np.pi
    azimuth = turn / cycle_length * (LANES * lane_r[None, :] + b[:, None] + 1)
    outer = turn / rows * (lane_r[:, None] * p[None, :] % rows)
    twist = turn / cycle_length * (b[:, None] * p[None, :] % cycle_length)
    inner = turn * ((LANES * u[:, None] * b[None, :]) % cycle_length) / cycle_length
    half_turn = turn / (2 * cycle_length) * (LANES * u[:, None] + p[None, :])
    f32 = np.float32
    parts = dict(
        cos_phi=np.cos(azimuth),
        sin_phi=np.sin(azimuth),
        outer_real=np.cos(outer),
        outer_imag=-np.sin(outer),
        twist_cos=np.cos(twist),
        twist_sin=np.sin(twist),
        inner_real=np.concatenate([np.cos(inner), -np.sin(inner)], 0),
        inner_imag=np.concatenate([np.sin(inner), np.cos(inner)], 0),
        half_cos=np.cos(half_turn),
        half_sin=np.sin(half_turn),
    )
    spans = {}
    top = 0
    for name, part in parts.items():
        spans[name] = slice(top, top + part.shape[0])
        top += part.shape[0]
    spans["rest"] = slice(spans["outer_real"].start, top)
    return np.concatenate(list(parts.values()), 0).astype(np.float32), spans


def placement(cycles, kinds, group):
    row = np.arange(cycles * kinds)[:, None]
    lane = np.arange(kinds * group * cycles)[None, :]
    same = (row % kinds == lane // (group * cycles)) & (row // kinds == lane % cycles)
    return jnp.asarray(same, jnp.bfloat16)


def early_shape(flat, owned):
    group = math.gcd(owned, GROUP)
    return (2, min(EARLY, owned // group) * group * (flat[0] // owned), flat[1])


def geometry_kernel(
    cycle, col, weight, order, table_hbm, a_hbm, b_hbm, place_hbm, col_t, weight_t, turn_cos, turn_sin,
    first_wave, rest, order_near, early, place, line, sems, *, spans, nside
):
    rows = early.shape[1]
    pieces = 4
    step = rows // pieces
    bulk = [pltpu.make_async_copy(place_hbm, place, sems.at[3])] + [
        pltpu.make_async_copy(
            source.at[pl.ds(i * step, step), :],
            early.at[which, pl.ds(i * step, step), :],
            sems.at[4 + which * pieces + i],
        )
        for i in range(pieces)
        for which, source in enumerate((a_hbm, b_hbm))
    ]
    cos_phi = pltpu.make_async_copy(table_hbm.at[spans["cos_phi"], :], turn_cos, sems.at[0])
    sin_phi = pltpu.make_async_copy(table_hbm.at[spans["sin_phi"], :], turn_sin, sems.at[1])
    other = pltpu.make_async_copy(table_hbm.at[spans["rest"], :], rest, sems.at[2])
    cos_phi.start()
    sin_phi.start()
    other.start()
    for copy in bulk:
        copy.start()
    col_t[...] = jnp.transpose(col[...])
    weight_t[...] = jnp.transpose(weight[...])
    order_near[...] = order[...]
    owned = first_wave.shape[0]
    slot = (lax.axis_index("band") * lax.axis_size("lev") + lax.axis_index("lev")) * owned
    mine = order[pl.ds(lax.div(slot, LANES), 1), :]
    line[...] = jnp.transpose(jnp.broadcast_to(mine, (LANES, LANES)))
    first_wave[...] = line[pl.ds(pl.multiple_of(lax.rem(slot, LANES), SUB), owned), :]
    half = lax.rem(cycle[0] - nside + 1, 2) != 0
    spacing = math.pi / (2.0 * nside)
    shift_cos = jnp.where(half, math.cos(0.5 * spacing), 1.0).astype(jnp.float32)
    shift_sin = jnp.where(half, math.sin(0.5 * spacing), 0.0).astype(jnp.float32)
    cos_phi.wait()
    sin_phi.wait()
    base_cos, base_sin = turn_cos[...], turn_sin[...]
    turn_cos[...] = base_cos * shift_cos + base_sin * shift_sin
    turn_sin[...] = base_sin * shift_cos - base_cos * shift_sin
    other.wait()
    for copy in bulk:
        copy.wait()


def cycle_geometry(
    cycle_ids, col, weight, order, owned, levels, split, cycle_length, table, spans, flat_a, flat_b
):
    cycles = flat_a.shape[0] // owned
    place = placement(cycles, levels * split, math.gcd(owned, GROUP))
    vmem = pl.BlockSpec(memory_space=pltpu.VMEM)
    square = (LANES, LANES)
    rest = spans["rest"].stop - spans["rest"].start
    return pl.pallas_call(
        functools.partial(
            geometry_kernel, spans=spans, nside=cycle_length // 4
        ),
        out_shape=(
            jax.ShapeDtypeStruct(square, jnp.int32),
            jax.ShapeDtypeStruct(square, jnp.float32),
            jax.ShapeDtypeStruct(square, jnp.float32),
            jax.ShapeDtypeStruct(square, jnp.float32),
            jax.ShapeDtypeStruct((owned, LANES), jnp.int32),
            jax.ShapeDtypeStruct((rest, LANES), jnp.float32),
            jax.ShapeDtypeStruct(order.shape, jnp.int32),
            jax.ShapeDtypeStruct(early_shape(flat_a.shape, owned), flat_a.dtype),
            jax.ShapeDtypeStruct(place.shape, place.dtype),
        ),
        in_specs=[pl.BlockSpec(memory_space=pltpu.SMEM), vmem, vmem, vmem]
        + [pl.BlockSpec(memory_space=pltpu.HBM)] * 4,
        out_specs=(vmem,) * 9,
        scratch_shapes=[pltpu.VMEM(square, jnp.int32), pltpu.SemaphoreType.DMA((12,))],
        compiler_params=pltpu.CompilerParams(vmem_limit_bytes=VMEM_ALL - ROOM),
        cost_estimate=pl.CostEstimate(flops=10**7, bytes_accessed=10**7, transcendentals=0),
        name="geometry",
    )(cycle_ids, *[far(x) for x in (col, weight, order, table, flat_a, flat_b, place)])


def halves(value):
    high = value.astype(jnp.bfloat16)
    return high, (value - high.astype(jnp.float32)).astype(jnp.bfloat16)


def product(left, right):
    return jnp.dot(left, right, preferred_element_type=jnp.float32)


def modes_kernel(
    cycle, received, col_t, weight_t, turn_cos, turn_sin, order, table, out, cart, field,
    *, spans, per, nside, paired
):
    components = cart.shape[0]
    span = components * per
    band_count = received.shape[0] // span
    tiles = LANES // SUB
    groups = band_count // SUB
    first = spans["rest"].start

    def part(name):
        return table[spans[name].start - first : spans[name].stop - first, :]

    for group in range(groups):
        block_rows = [
            [
                received[pl.ds(group * SUB * span + comp * per + blk, SUB, stride=span), :]
                for blk in range(per)
            ]
            for comp in range(components)
        ]
        for tile in range(group, tiles, groups):
            rows = slice(tile * SUB, (tile + 1) * SUB)
            index = col_t[rows, :]
            lane = index & (BLK - 1)
            block = index >> (BLK.bit_length() - 1)
            values = [jnp.take_along_axis(part_rows[0], lane, axis=1) for part_rows in block_rows]
            for blk in range(1, per):
                here = block == blk
                for comp in range(components):
                    found = jnp.take_along_axis(block_rows[comp][blk], lane, axis=1)
                    values[comp] = jnp.where(here, found, values[comp])
            for comp in range(components):
                cart[comp, rows, :] = values[comp] * weight_t[rows, :]
    number = cycle[0]
    half = lax.rem(number - nside + 1, 2) != 0
    number_f = jnp.full((SUB, LANES), number, jnp.int32).astype(jnp.float32)
    cos_tile = 4.0 / 3.0 - 2.0 * number_f / (3.0 * nside)
    sin_tile = jnp.sqrt(1.0 - cos_tile * cos_tile)
    cos_theta = cos_tile[:1, :]
    sin_theta = sin_tile[:1, :]
    cos_phi, sin_phi = turn_cos[...], turn_sin[...]
    x, y, z = cart[0], cart[1], cart[2]
    east = cos_phi * y - sin_phi * x
    north = sin_theta * z - cos_theta * (cos_phi * x + sin_phi * y)
    samples = jnp.concatenate([east, north], axis=0)
    outer = jnp.concatenate([part("outer_real"), part("outer_imag")], axis=1)
    outer_high, outer_low = halves(outer)
    high, low = halves(samples)
    section = product(
        jnp.concatenate([high, low, high], axis=1),
        jnp.concatenate([outer_high, outer_high, outer_low], axis=0),
    )
    twist_cos, twist_sin = part("twist_cos"), part("twist_sin")
    turned_real = []
    turned_imag = []
    for f in range(2):
        real = section[f * LANES : (f + 1) * LANES, :LANES]
        imag = section[f * LANES : (f + 1) * LANES, LANES:]
        turned_real.append(real * twist_cos + imag * twist_sin)
        turned_imag.append(imag * twist_cos - real * twist_sin)
    turned = jnp.concatenate(
        [jnp.concatenate(turned_real, axis=1), jnp.concatenate(turned_imag, axis=1)], axis=0
    )
    inner = jnp.concatenate([part("inner_real"), part("inner_imag")], axis=1)
    rows = field.shape[1]
    inner_high, inner_low = halves(inner)
    high, low = halves(turned)
    both = product(jnp.concatenate([inner_high, inner_low], axis=0), high)
    spectrum = both[: 2 * rows] + both[2 * rows :] + product(inner_high, low)
    half_cos, half_sin = part("half_cos"), part("half_sin")
    rot_cos = jnp.where(half, half_cos, half_cos * half_cos - half_sin * half_sin)
    rot_sin = jnp.where(half, half_sin, 2.0 * half_cos * half_sin)
    for f in range(2):
        real = spectrum[:rows, f * LANES : (f + 1) * LANES]
        imag = spectrum[rows:, f * LANES : (f + 1) * LANES]
        field[2 * f] = real * rot_cos + imag * rot_sin
        field[2 * f + 1] = imag * rot_cos - real * rot_sin
    front = lax.broadcasted_iota(jnp.int32, (SUB, LANES), 1) < LANES // 2
    for top in range(0, rows, SUB):
        wave = order[top : top + SUB, :]
        lane = wave & (LANES - 1)
        block = wave >> (LANES.bit_length() - 1)
        picked = []
        for k in range(4):
            value = None
            for blk in range(rows):
                source = jnp.broadcast_to(field[k, blk : blk + 1, :], (SUB, LANES))
                found = jnp.take_along_axis(source, lane, axis=1)
                value = found if value is None else jnp.where(block == blk, found, value)
            picked.append(value.astype(jnp.bfloat16).astype(jnp.float32))
        if paired:
            for h in range(2):
                first_f, second_f = picked[2 * h], picked[2 * h + 1]
                out[top : top + SUB, h, :] = jnp.where(
                    front, first_f, pltpu.roll(second_f, LANES // 2, axis=1)
                )
                out[top : top + SUB, 2 + h, :] = jnp.where(
                    front, pltpu.roll(first_f, LANES // 2, axis=1), second_f
                )
        else:
            for k in range(4):
                out[top : top + SUB, k, :] = picked[k]


def cycle_modes(cycle_ids, received, geometry, components, cycle_length, per, paired, spans):
    col_t, weight_t, turn_cos, turn_sin, _, rest, order, _, _ = geometry
    rows = order.shape[0]
    vmem = pl.BlockSpec(memory_space=pltpu.VMEM)
    return pl.pallas_call(
        functools.partial(
            modes_kernel, spans=spans, per=per, nside=cycle_length // 4, paired=paired
        ),
        out_shape=jax.ShapeDtypeStruct((rows, 4, LANES), jnp.float32),
        in_specs=[pl.BlockSpec(memory_space=pltpu.SMEM)] + [vmem] * 7,
        out_specs=vmem,
        scratch_shapes=[
            pltpu.VMEM((components, LANES, LANES), jnp.float32),
            pltpu.VMEM((4, rows, LANES), jnp.float32),
        ],
        compiler_params=pltpu.CompilerParams(vmem_limit_bytes=VMEM_ALL - ROOM),
        name="modes",
    )(cycle_ids, received, col_t, weight_t, turn_cos, turn_sin, order, rest)


PARTS = ((-1, 1, -1, 2), (1, 0, -1, 3), (-1, 3, 1, 0), (1, 2, 1, 1))


def legendre_kernel(
    modes, first_wave, early, place, a_hbm, b_hbm, div_hbm, vort_hbm, table_a, table_b, turned, div, vort,
    in_sems, out_sems, *, levels, cycles, group, split
):
    owned = turned.shape[0] * split // 4
    width = group * cycles
    groups = owned // group
    degrees = table_a.shape[1]

    def fetch(g, which):
        source, target = ((a_hbm, table_a), (b_hbm, table_b))[which]
        rows = pl.ds(g * width, width)
        return pltpu.make_async_copy(source.at[rows, :], target.at[rows, :], in_sems.at[g, which])

    def flush(g, which):
        source, target = ((div, div_hbm), (vort, vort_hbm))[which]
        rows = pl.ds(g * group, group)
        return pltpu.make_async_copy(
            source.at[:, :, rows, :], target.at[:, :, rows, :], out_sems.at[g, which]
        )

    ready = early.shape[1] // width
    for g in range(ready, groups):
        for which in range(2):
            fetch(g, which).start()
    turned[...] = jnp.transpose(modes[...])
    slot = lax.broadcasted_iota(jnp.int32, (group, width), 0)
    entry = lax.broadcasted_iota(jnp.int32, (group, width), 1)
    own = slot == lax.div(entry, cycles)
    fields = 4 // split
    chunk = min(256, degrees)
    def one_group(g, tables_of, late):
        base = pl.multiple_of(g * group, group)
        mine = jnp.concatenate(
            [turned[pl.ds(i * owned + base, group), :] for i in range(fields)], axis=0
        ).astype(jnp.bfloat16)
        wide = jnp.dot(mine, place[...], preferred_element_type=jnp.float32)

        def spread(f, lev, sign):
            h, i = divmod(f, fields)
            start = (lev * split + h) * width
            part = wide[i * group : (i + 1) * group, start : start + width]
            return jnp.where(own, part if sign > 0 else -part, 0.0)

        mix = jnp.concatenate(
            [
                jnp.concatenate(
                    [spread(field_a, lev, sign_a), spread(field_b, lev, sign_b)], axis=1
                )
                for sign_a, field_a, sign_b, field_b in PARTS
                for lev in range(levels)
            ],
            axis=0,
        ).astype(jnp.bfloat16)
        waves = first_wave[pl.ds(base, group), :]
        if late:
            fetch(g, 0).wait()
            fetch(g, 1).wait()
        for start in range(0, degrees, chunk):
            at_rows = pl.ds(pl.multiple_of(g * width, width), width)
            lanes = slice(start, start + chunk)
            both = jnp.concatenate([table[at_rows, lanes] for table in tables_of], axis=0)
            result = jnp.dot(mix, both, preferred_element_type=jnp.float32)
            for at in range(0, chunk, LANES):
                degree = lax.broadcasted_iota(jnp.int32, (group, LANES), 1) + (start + at)
                upper = degree >= waves
                for part in range(4):
                    target = div if part < 2 else vort
                    for lev in range(levels):
                        top = (part * levels + lev) * group
                        lanes = slice(start + at, start + at + LANES)
                        target[part % 2, lev, pl.ds(base, group), lanes] = jnp.where(
                            upper, result[top : top + group, at : at + LANES], 0.0
                        )
        flush(g, 0).start()
        flush(g, 1).start()
    def ready_group(g, carry):
        one_group(g, (early.at[0], early.at[1]), False)
        return carry

    def late_group(g, carry):
        one_group(g, (table_a, table_b), True)
        return carry

    lax.fori_loop(0, ready, ready_group, 0)
    lax.fori_loop(ready, groups, late_group, 0)
    for g in range(groups):
        flush(g, 0).wait()
        flush(g, 1).wait()


def legendre_sums(modes, first_wave, early, place, flat_a, flat_b, owned, levels, split):
    flat = flat_a.shape
    cycles, degrees = flat[0] // owned, flat[1]
    group = math.gcd(owned, GROUP)
    full = (2, levels, owned, degrees)
    out_shape = jax.ShapeDtypeStruct(full, jnp.float32)
    vmem = pl.BlockSpec(memory_space=pltpu.VMEM)
    hbm = pl.BlockSpec(memory_space=pltpu.HBM)
    return pl.pallas_call(
        functools.partial(
            legendre_kernel, levels=levels, cycles=cycles, group=group, split=split
        ),
        out_shape=(out_shape, out_shape),
        in_specs=[vmem, vmem, vmem, vmem, hbm, hbm],
        out_specs=(hbm, hbm),
        scratch_shapes=[
            pltpu.VMEM(flat, jnp.bfloat16),
            pltpu.VMEM(flat, jnp.bfloat16),
            pltpu.VMEM(modes.shape[::-1], jnp.float32),
            pltpu.VMEM(full, jnp.float32),
            pltpu.VMEM(full, jnp.float32),
            pltpu.SemaphoreType.DMA((owned // group, 2)),
            pltpu.SemaphoreType.DMA((owned // group, 2)),
        ],
        compiler_params=pltpu.CompilerParams(vmem_limit_bytes=VMEM_ALL - ROOM),
        name="legendre",
    )(modes, first_wave, early, place, far(flat_a), far(flat_b))


def local(winds, remap_w, remap_col, block_pick, cycle_ids, wave_ids, legendre_a, legendre_b):
    band_count = lax.axis_size("band")
    level_count = lax.axis_size("lev")
    components, levels_dev, column_count = winds.shape
    taps, cycle_count, cycle_length = remap_col.shape
    per = block_pick.shape[1] // band_count
    waves = wave_ids.shape[0]
    devices = band_count * level_count
    owned = waves // devices
    assert levels_dev == 1 and cycle_count == 1
    assert taps * cycle_length == LANES * LANES and band_count % SUB == 0
    blocks = winds.reshape(components, column_count // BLK, BLK)
    outgoing = pick_blocks(block_pick, blocks, band_count, per)
    received = lax.all_to_all(outgoing, "band", split_axis=0, concat_axis=0, tiled=True)
    received = received.reshape(band_count * components * per, BLK)
    paired = 2 * owned == LANES
    split = 2 if paired else 1
    flat_a = legendre_a.reshape(-1, legendre_a.shape[2])
    flat_b = legendre_b.reshape(-1, legendre_b.shape[2])
    table, spans = tables(cycle_length, taps, waves)
    order = wave_ids.reshape(waves // LANES, LANES)
    geometry = cycle_geometry(
        cycle_ids,
        remap_col.reshape(LANES, LANES),
        remap_w.reshape(LANES, LANES),
        order,
        owned,
        level_count,
        split,
        cycle_length,
        jnp.asarray(table),
        spans,
        flat_a,
        flat_b,
    )
    chosen = cycle_modes(
        cycle_ids, received, geometry, components, cycle_length, per, paired, spans
    )
    if paired:
        parcels = chosen.reshape(devices, split, LANES)
    else:
        parcels = jnp.transpose(
            jnp.transpose(chosen.reshape(-1, 4, LANES), (1, 0, 2)).reshape(4, devices, owned), (1, 0, 2)
        ).reshape(devices, 1, 4 * owned)
    gathered = lax.all_to_all(parcels, ("band", "lev"), split_axis=0, concat_axis=0, tiled=True)
    modes = gathered.reshape(devices * split, 4 * owned // split)
    return legendre_sums(
        modes, geometry[4], geometry[7], geometry[8], flat_a, flat_b, owned, level_count, split
    )


def solution(mesh):
    placed = (
        P(None, "lev", "band"),
        P(None, "band", None),
        P(None, "band", None),
        P(),
        P("band"),
        P(),
        P(("band", "lev"), None, None),
        P(("band", "lev"), None, None),
    )
    return jax.shard_map(
        local,
        mesh=mesh,
        in_specs=placed,
        out_specs=(P(None, None, ("band", "lev"), None), P(None, None, ("band", "lev"), None)),
        check_vma=False,
    )
```

```python
import functools
import math

import jax
import jax.numpy as jnp
import numpy as np
from jax import lax
from jax.experimental import pallas as pl
from jax.experimental.pallas import tpu as pltpu
from jax.sharding import PartitionSpec as P

BLK = 128
LANES = 128
SUB = 8
SHARES = 2
GROUP = 16
EARLY = 2
VMEM_ALL = 67043328
ROOM = 24000 * 1024


def far(array):
    return pltpu.with_memory_space_constraint(array, pltpu.HBM)


def pick_kernel(picks, winds, out, *, per):
    band = lax.axis_index("band")
    components = winds.shape[0]

    def one_target(t, carry):
        for c in range(per):
            block = picks[t, band * per + c]
            for comp in range(components):
                place, row = divmod(comp * per + c, out.shape[2])
                out[t, place, pl.ds(row, 1), :] = winds[comp, pl.ds(block, 1), :]
        return carry

    lax.fori_loop(0, out.shape[0], one_target, 0, unroll=out.shape[0] <= 8)


def pick_blocks(block_pick, winds, band_count, per):
    components, blocks, _ = winds.shape
    quad = math.gcd(components * per, 4)
    return pl.pallas_call(
        functools.partial(pick_kernel, per=per),
        out_shape=jax.ShapeDtypeStruct(
            (band_count, components * per // quad, quad, BLK), winds.dtype
        ),
        in_specs=[
            pl.BlockSpec(memory_space=pltpu.SMEM),
            pl.BlockSpec(memory_space=pltpu.VMEM),
        ],
        out_specs=pl.BlockSpec(memory_space=pltpu.VMEM),
        compiler_params=pltpu.CompilerParams(vmem_limit_bytes=VMEM_ALL - ROOM),
        name="pick",
    )(far(block_pick), far(winds))


@functools.lru_cache(maxsize=None)
def tables(cycle_length, taps, waves):
    rows = cycle_length // LANES
    b = np.arange(LANES, dtype=np.int64)
    lane_r = np.arange(taps * rows, dtype=np.int64) % rows
    p = np.arange(LANES, dtype=np.int64)
    u = np.arange(waves // LANES, dtype=np.int64)
    turn = 2.0 * np.pi
    azimuth = turn / cycle_length * (LANES * lane_r[None, :] + b[:, None] + 1)
    outer = turn / rows * (lane_r[:, None] * p[None, :] % rows)
    twist = turn / cycle_length * (b[:, None] * p[None, :] % cycle_length)
    inner = turn * ((LANES * u[:, None] * b[None, :]) % cycle_length) / cycle_length
    half_turn = turn / (2 * cycle_length) * (LANES * u[:, None] + p[None, :])
    f32 = np.float32
    parts = dict(
        cos_phi=np.cos(azimuth),
        sin_phi=np.sin(azimuth),
        outer_real=np.cos(outer),
        outer_imag=-np.sin(outer),
        twist_cos=np.cos(twist),
        twist_sin=np.sin(twist),
        inner_real=np.concatenate([np.cos(inner), -np.sin(inner)], 0),
        inner_imag=np.concatenate([np.sin(inner), np.cos(inner)], 0),
        half_cos=np.cos(half_turn),
        half_sin=np.sin(half_turn),
    )
    spans = {}
    top = 0
    for name, part in parts.items():
        spans[name] = slice(top, top + part.shape[0])
        top += part.shape[0]
    spans["rest"] = slice(spans["outer_real"].start, top)
    return np.concatenate(list(parts.values()), 0).astype(np.float32), spans


def placement(cycles, kinds, group):
    row = np.arange(cycles * kinds)[:, None]
    lane = np.arange(kinds * group * cycles)[None, :]
    same = (row % kinds == lane // (group * cycles)) & (row // kinds == lane % cycles)
    return jnp.asarray(same, jnp.bfloat16)


def early_shape(flat, owned):
    group = math.gcd(owned, GROUP)
    return (2, min(EARLY, owned // group) * group * (flat[0] // owned), flat[1])


def geometry_kernel(
    cycle, col, weight, order, table_hbm, a_hbm, b_hbm, place_hbm, col_t, weight_t, turn_cos, turn_sin,
    first_wave, rest, order_near, early, place, line, sems, *, spans, nside
):
    rows = early.shape[1]
    pieces = 4
    step = rows // pieces
    bulk = [pltpu.make_async_copy(place_hbm, place, sems.at[3])] + [
        pltpu.make_async_copy(
            source.at[pl.ds(i * step, step), :],
            early.at[which, pl.ds(i * step, step), :],
            sems.at[4 + which * pieces + i],
        )
        for i in range(pieces)
        for which, source in enumerate((a_hbm, b_hbm))
    ]
    cos_phi = pltpu.make_async_copy(table_hbm.at[spans["cos_phi"], :], turn_cos, sems.at[0])
    sin_phi = pltpu.make_async_copy(table_hbm.at[spans["sin_phi"], :], turn_sin, sems.at[1])
    other = pltpu.make_async_copy(table_hbm.at[spans["rest"], :], rest, sems.at[2])
    cos_phi.start()
    sin_phi.start()
    other.start()
    for copy in bulk:
        copy.start()
    col_t[...] = jnp.transpose(col[...])
    weight_t[...] = jnp.transpose(weight[...])
    order_near[...] = order[...]
    owned = first_wave.shape[0]
    slot = (lax.axis_index("band") * lax.axis_size("lev") + lax.axis_index("lev")) * owned
    mine = order[pl.ds(lax.div(slot, LANES), 1), :]
    line[...] = jnp.transpose(jnp.broadcast_to(mine, (LANES, LANES)))
    first_wave[...] = line[pl.ds(pl.multiple_of(lax.rem(slot, LANES), SUB), owned), :]
    half = lax.rem(cycle[0] - nside + 1, 2) != 0
    spacing = math.pi / (2.0 * nside)
    shift_cos = jnp.where(half, math.cos(0.5 * spacing), 1.0).astype(jnp.float32)
    shift_sin = jnp.where(half, math.sin(0.5 * spacing), 0.0).astype(jnp.float32)
    cos_phi.wait()
    sin_phi.wait()
    base_cos, base_sin = turn_cos[...], turn_sin[...]
    turn_cos[...] = base_cos * shift_cos + base_sin * shift_sin
    turn_sin[...] = base_sin * shift_cos - base_cos * shift_sin
    other.wait()
    for copy in bulk:
        copy.wait()


def cycle_geometry(
    cycle_ids, col, weight, order, owned, levels, split, cycle_length, table, spans, flat_a, flat_b
):
    cycles = flat_a.shape[0] // owned
    place = placement(cycles, levels * split, math.gcd(owned, GROUP))
    vmem = pl.BlockSpec(memory_space=pltpu.VMEM)
    square = (LANES, LANES)
    rest = spans["rest"].stop - spans["rest"].start
    return pl.pallas_call(
        functools.partial(
            geometry_kernel, spans=spans, nside=cycle_length // 4
        ),
        out_shape=(
            jax.ShapeDtypeStruct(square, jnp.int32),
            jax.ShapeDtypeStruct(square, jnp.float32),
            jax.ShapeDtypeStruct(square, jnp.float32),
            jax.ShapeDtypeStruct(square, jnp.float32),
            jax.ShapeDtypeStruct((owned, LANES), jnp.int32),
            jax.ShapeDtypeStruct((rest, LANES), jnp.float32),
            jax.ShapeDtypeStruct(order.shape, jnp.int32),
            jax.ShapeDtypeStruct(early_shape(flat_a.shape, owned), flat_a.dtype),
            jax.ShapeDtypeStruct(place.shape, place.dtype),
        ),
        in_specs=[pl.BlockSpec(memory_space=pltpu.SMEM), vmem, vmem, vmem]
        + [pl.BlockSpec(memory_space=pltpu.HBM)] * 4,
        out_specs=(vmem,) * 9,
        scratch_shapes=[pltpu.VMEM(square, jnp.int32), pltpu.SemaphoreType.DMA((12,))],
        compiler_params=pltpu.CompilerParams(vmem_limit_bytes=VMEM_ALL - ROOM),
        cost_estimate=pl.CostEstimate(flops=10**7, bytes_accessed=10**7, transcendentals=0),
        name="geometry",
    )(cycle_ids, *[far(x) for x in (col, weight, order, table, flat_a, flat_b, place)])


def halves(value):
    high = value.astype(jnp.bfloat16)
    return high, (value - high.astype(jnp.float32)).astype(jnp.bfloat16)


def product(left, right):
    return jnp.dot(left, right, preferred_element_type=jnp.float32)


def modes_kernel(
    cycle, received, col_t, weight_t, turn_cos, turn_sin, order, table, out, cart, field,
    *, spans, per, nside, paired
):
    components = cart.shape[0]
    span = components * per
    band_count = received.shape[0] // span
    tiles = LANES // SUB
    groups = band_count // SUB
    first = spans["rest"].start

    def part(name):
        return table[spans[name].start - first : spans[name].stop - first, :]

    number = cycle[0]
    half = lax.rem(number - nside + 1, 2) != 0
    number_f = jnp.full((SUB, LANES), number, jnp.int32).astype(jnp.float32)
    cos_tile = 4.0 / 3.0 - 2.0 * number_f / (3.0 * nside)
    sin_tile = jnp.sqrt(1.0 - cos_tile * cos_tile)
    cos_theta = cos_tile[:1, :]
    sin_theta = sin_tile[:1, :]
    outer = jnp.concatenate([part("outer_real"), part("outer_imag")], axis=1)
    outer_high, outer_low = halves(outer)
    outer_all = jnp.concatenate([outer_high, outer_high, outer_low], axis=0)
    twist_cos, twist_sin = part("twist_cos"), part("twist_sin")
    share = LANES // SHARES
    turned_real = [[], []]
    turned_imag = [[], []]
    for first_row in range(0, LANES, share):
        for tile in range(first_row // SUB, (first_row + share) // SUB):
            group = tile % groups
            rows = slice(tile * SUB, (tile + 1) * SUB)
            index = col_t[rows, :]
            lane = index & (BLK - 1)
            block = index >> (BLK.bit_length() - 1)
            values = [None] * components
            for blk in range(per):
                here = block == blk
                for comp in range(components):
                    row = group * SUB * span + comp * per + blk
                    table_rows = received[pl.ds(row, SUB, stride=span), :]
                    found = jnp.take_along_axis(table_rows, lane, axis=1)
                    values[comp] = found if blk == 0 else jnp.where(here, found, values[comp])
            for comp in range(components):
                cart[comp, rows, :] = values[comp] * weight_t[rows, :]
        rows = slice(first_row, first_row + share)
        cos_phi, sin_phi = turn_cos[rows, :], turn_sin[rows, :]
        x, y, z = cart[0, rows, :], cart[1, rows, :], cart[2, rows, :]
        east = cos_phi * y - sin_phi * x
        north = sin_theta * z - cos_theta * (cos_phi * x + sin_phi * y)
        high, low = halves(jnp.concatenate([east, north], axis=0))
        section = product(jnp.concatenate([high, low, high], axis=1), outer_all)
        for f in range(2):
            real = section[f * share : (f + 1) * share, :LANES]
            imag = section[f * share : (f + 1) * share, LANES:]
            turned_real[f].append(real * twist_cos[rows] + imag * twist_sin[rows])
            turned_imag[f].append(imag * twist_cos[rows] - real * twist_sin[rows])
    turned = jnp.concatenate(
        [
            jnp.concatenate([jnp.concatenate(pieces, axis=0) for pieces in kind], axis=1)
            for kind in (turned_real, turned_imag)
        ],
        axis=0,
    )
    inner = jnp.concatenate([part("inner_real"), part("inner_imag")], axis=1)
    rows = field.shape[1]
    inner_high, inner_low = halves(inner)
    high, low = halves(turned)
    both = product(jnp.concatenate([inner_high, inner_low], axis=0), high)
    spectrum = both[: 2 * rows] + both[2 * rows :] + product(inner_high, low)
    half_cos, half_sin = part("half_cos"), part("half_sin")
    rot_cos = jnp.where(half, half_cos, half_cos * half_cos - half_sin * half_sin)
    rot_sin = jnp.where(half, half_sin, 2.0 * half_cos * half_sin)
    for f in range(2):
        real = spectrum[:rows, f * LANES : (f + 1) * LANES]
        imag = spectrum[rows:, f * LANES : (f + 1) * LANES]
        field[2 * f] = real * rot_cos + imag * rot_sin
        field[2 * f + 1] = imag * rot_cos - real * rot_sin
    front = lax.broadcasted_iota(jnp.int32, (SUB, LANES), 1) < LANES // 2
    for top in range(0, rows, SUB):
        wave = order[top : top + SUB, :]
        lane = wave & (LANES - 1)
        block = wave >> (LANES.bit_length() - 1)
        picked = []
        for k in range(4):
            value = None
            for blk in range(rows):
                source = jnp.broadcast_to(field[k, blk : blk + 1, :], (SUB, LANES))
                found = jnp.take_along_axis(source, lane, axis=1)
                value = found if value is None else jnp.where(block == blk, found, value)
            picked.append(value.astype(jnp.bfloat16).astype(jnp.float32))
        if paired:
            for h in range(2):
                first_f, second_f = picked[2 * h], picked[2 * h + 1]
                out[top : top + SUB, h, :] = jnp.where(
                    front, first_f, pltpu.roll(second_f, LANES // 2, axis=1)
                )
                out[top : top + SUB, 2 + h, :] = jnp.where(
                    front, pltpu.roll(first_f, LANES // 2, axis=1), second_f
                )
        else:
            for k in range(4):
                out[top : top + SUB, k, :] = picked[k]


def cycle_modes(cycle_ids, received, geometry, components, cycle_length, per, paired, spans):
    col_t, weight_t, turn_cos, turn_sin, _, rest, order, _, _ = geometry
    rows = order.shape[0]
    vmem = pl.BlockSpec(memory_space=pltpu.VMEM)
    return pl.pallas_call(
        functools.partial(
            modes_kernel, spans=spans, per=per, nside=cycle_length // 4, paired=paired
        ),
        out_shape=jax.ShapeDtypeStruct((rows, 4, LANES), jnp.float32),
        in_specs=[pl.BlockSpec(memory_space=pltpu.SMEM)] + [vmem] * 7,
        out_specs=vmem,
        scratch_shapes=[
            pltpu.VMEM((components, LANES, LANES), jnp.float32),
            pltpu.VMEM((4, rows, LANES), jnp.float32),
        ],
        compiler_params=pltpu.CompilerParams(vmem_limit_bytes=VMEM_ALL - ROOM),
        name="modes",
    )(cycle_ids, received, col_t, weight_t, turn_cos, turn_sin, order, rest)


PARTS = ((-1, 1, -1, 2), (1, 0, -1, 3), (-1, 3, 1, 0), (1, 2, 1, 1))


def legendre_kernel(
    modes, first_wave, early, place, a_hbm, b_hbm, div_hbm, vort_hbm, table_a, table_b, turned, div, vort,
    in_sems, out_sems, *, levels, cycles, group, split
):
    owned = turned.shape[0] * split // 4
    width = group * cycles
    groups = owned // group
    degrees = table_a.shape[1]

    def fetch(g, which):
        source, target = ((a_hbm, table_a), (b_hbm, table_b))[which]
        rows = pl.ds(g * width, width)
        return pltpu.make_async_copy(source.at[rows, :], target.at[rows, :], in_sems.at[g, which])

    def flush(g, which):
        source, target = ((div, div_hbm), (vort, vort_hbm))[which]
        rows = pl.ds(g * group, group)
        return pltpu.make_async_copy(
            source.at[:, :, rows, :], target.at[:, :, rows, :], out_sems.at[g, which]
        )

    ready = early.shape[1] // width
    for g in range(ready, groups):
        for which in range(2):
            fetch(g, which).start()
    turned[...] = jnp.transpose(modes[...])
    slot = lax.broadcasted_iota(jnp.int32, (group, width), 0)
    entry = lax.broadcasted_iota(jnp.int32, (group, width), 1)
    own = slot == lax.div(entry, cycles)
    fields = 4 // split
    chunk = min(256, degrees)
    for g in range(groups):
        base = g * group
        mine = jnp.concatenate(
            [turned[i * owned + base : i * owned + base + group, :] for i in range(fields)], axis=0
        ).astype(jnp.bfloat16)
        wide = jnp.dot(mine, place[...], preferred_element_type=jnp.float32)

        def spread(f, lev, sign):
            h, i = divmod(f, fields)
            start = (lev * split + h) * width
            part = wide[i * group : (i + 1) * group, start : start + width]
            return jnp.where(own, part if sign > 0 else -part, 0.0)

        mix = jnp.concatenate(
            [
                jnp.concatenate(
                    [spread(field_a, lev, sign_a), spread(field_b, lev, sign_b)], axis=1
                )
                for sign_a, field_a, sign_b, field_b in PARTS
                for lev in range(levels)
            ],
            axis=0,
        ).astype(jnp.bfloat16)
        waves = first_wave[base : base + group, :]
        if g >= ready:
            fetch(g, 0).wait()
            fetch(g, 1).wait()
        for start in range(0, degrees, chunk):
            at_rows = slice(g * width, (g + 1) * width)
            lanes = slice(start, start + chunk)
            if g < ready:
                both = jnp.concatenate([early[0, at_rows, lanes], early[1, at_rows, lanes]], axis=0)
            else:
                both = jnp.concatenate([table_a[at_rows, lanes], table_b[at_rows, lanes]], axis=0)
            result = jnp.dot(mix, both, preferred_element_type=jnp.float32)
            for at in range(0, chunk, LANES):
                degree = lax.broadcasted_iota(jnp.int32, (group, LANES), 1) + (start + at)
                upper = degree >= waves
                for part in range(4):
                    target = div if part < 2 else vort
                    for lev in range(levels):
                        top = (part * levels + lev) * group
                        lanes = slice(start + at, start + at + LANES)
                        target[part % 2, lev, base : base + group, lanes] = jnp.where(
                            upper, result[top : top + group, at : at + LANES], 0.0
                        )
        flush(g, 0).start()
        flush(g, 1).start()
    for g in range(groups):
        flush(g, 0).wait()
        flush(g, 1).wait()


def legendre_sums(modes, first_wave, early, place, flat_a, flat_b, owned, levels, split):
    flat = flat_a.shape
    cycles, degrees = flat[0] // owned, flat[1]
    group = math.gcd(owned, GROUP)
    full = (2, levels, owned, degrees)
    out_shape = jax.ShapeDtypeStruct(full, jnp.float32)
    vmem = pl.BlockSpec(memory_space=pltpu.VMEM)
    hbm = pl.BlockSpec(memory_space=pltpu.HBM)
    return pl.pallas_call(
        functools.partial(
            legendre_kernel, levels=levels, cycles=cycles, group=group, split=split
        ),
        out_shape=(out_shape, out_shape),
        in_specs=[vmem, vmem, vmem, vmem, hbm, hbm],
        out_specs=(hbm, hbm),
        scratch_shapes=[
            pltpu.VMEM(flat, jnp.bfloat16),
            pltpu.VMEM(flat, jnp.bfloat16),
            pltpu.VMEM(modes.shape[::-1], jnp.float32),
            pltpu.VMEM(full, jnp.float32),
            pltpu.VMEM(full, jnp.float32),
            pltpu.SemaphoreType.DMA((owned // group, 2)),
            pltpu.SemaphoreType.DMA((owned // group, 2)),
        ],
        compiler_params=pltpu.CompilerParams(vmem_limit_bytes=VMEM_ALL - ROOM),
        name="legendre",
    )(modes, first_wave, early, place, far(flat_a), far(flat_b))


def local(winds, remap_w, remap_col, block_pick, cycle_ids, wave_ids, legendre_a, legendre_b):
    band_count = lax.axis_size("band")
    level_count = lax.axis_size("lev")
    components, levels_dev, column_count = winds.shape
    taps, cycle_count, cycle_length = remap_col.shape
    per = block_pick.shape[1] // band_count
    waves = wave_ids.shape[0]
    devices = band_count * level_count
    owned = waves // devices
    assert levels_dev == 1 and cycle_count == 1
    assert taps * cycle_length == LANES * LANES and band_count % SUB == 0
    blocks = winds.reshape(components, column_count // BLK, BLK)
    outgoing = pick_blocks(block_pick, blocks, band_count, per)
    received = lax.all_to_all(outgoing, "band", split_axis=0, concat_axis=0, tiled=True)
    received = received.reshape(band_count * components * per, BLK)
    paired = 2 * owned == LANES
    split = 2 if paired else 1
    flat_a = legendre_a.reshape(-1, legendre_a.shape[2])
    flat_b = legendre_b.reshape(-1, legendre_b.shape[2])
    table, spans = tables(cycle_length, taps, waves)
    order = wave_ids.reshape(waves // LANES, LANES)
    geometry = cycle_geometry(
        cycle_ids,
        remap_col.reshape(LANES, LANES),
        remap_w.reshape(LANES, LANES),
        order,
        owned,
        level_count,
        split,
        cycle_length,
        jnp.asarray(table),
        spans,
        flat_a,
        flat_b,
    )
    chosen = cycle_modes(
        cycle_ids, received, geometry, components, cycle_length, per, paired, spans
    )
    if paired:
        parcels = chosen.reshape(devices, split, LANES)
    else:
        parcels = jnp.transpose(
            jnp.transpose(chosen.reshape(-1, 4, LANES), (1, 0, 2)).reshape(4, devices, owned), (1, 0, 2)
        ).reshape(devices, 1, 4 * owned)
    gathered = lax.all_to_all(parcels, ("band", "lev"), split_axis=0, concat_axis=0, tiled=True)
    modes = gathered.reshape(devices * split, 4 * owned // split)
    return legendre_sums(
        modes, geometry[4], geometry[7], geometry[8], flat_a, flat_b, owned, level_count, split
    )


def solution(mesh):
    placed = (
        P(None, "lev", "band"),
        P(None, "band", None),
        P(None, "band", None),
        P(),
        P("band"),
        P(),
        P(("band", "lev"), None, None),
        P(("band", "lev"), None, None),
    )
    return jax.shard_map(
        local,
        mesh=mesh,
        in_specs=placed,
        out_specs=(P(None, None, ("band", "lev"), None), P(None, None, ("band", "lev"), None)),
        check_vma=False,
    )
```
